512 devices in a mesh: grp: 16 (over y, z_hi, core), dev: 32 (over x, z_lo).
Axes of the slice: x: 4, y: 4, z: 16 (z_hi: 2, z_lo: 8; z = z_hi * 8 + z_lo), core: 2. Of those that a mesh axis runs over, the one named last changes fastest.
Arguments:
- colloc: bfloat16 [12288, 8000], P('dev', 'grp'), may hold values from -3 to 3
- block_colloc: bfloat16 [1024, 8000], P('dev', 'grp'), may hold values from -3 to 3
- factor: float32 [12288, 8192], P('dev', 'grp'), may hold values from -4.8 to 4.8
- block_factor: float32 [1024, 8192], P('dev', 'grp'), may hold values from -0.25 to 0.25
Outputs:
- block_lower: float32 [1024, 1024], P('dev')
- panel_lower: float32 [32, 384, 1024], P('dev', 'grp')
The draws below stay inside these ranges and needn't reach their ends.
All inputs are finite; a program needn't handle non-finite values.
Results may differ from the reference program's by a relative error of at most 0.0003.
Values may be sent and summed in bfloat16 or wider, within the bound.
A program may use at most 64 MiB of HBM per device.

```python
import math
import jax
import jax.numpy as jnp
from jax import lax

NORB = 8000
PANEL_COLUMNS = 1024
FINISHED_COLUMNS = 8192
RB = 384
BANDS = 32
ROWS = 12288


NOISE_SHARE = 0.1


LOW_SCALE = 1.2


def orbital_terms(key):
    centers = jax.random.uniform(jax.random.fold_in(key, 7), (NORB,), jnp.float32, 0.0, 1.0)
    scales = jnp.exp(jax.random.uniform(jax.random.fold_in(key, 8), (NORB,), jnp.float32, -1.5, 1.5))
    amplitude = jnp.clip(jax.random.normal(jax.random.fold_in(key, 9), (NORB,), jnp.float32), -2.5, 2.5)
    return (centers, scales, amplitude)


def collocation(key, count_of_rows, salt_value):
    starting_key = jax.random.fold_in(key, salt_value)
    position_key, noise_key, row_key = jax.random.split(starting_key, 3)
    centers, scales, amplitude = orbital_terms(key)
    kernel_width = min(24.0 / PANEL_COLUMNS, 0.08)
    positions = jax.random.uniform(position_key, (count_of_rows, 1), jnp.float32, 0.0, 1.0)
    offset = positions - centers[None, :]
    offset = offset - jnp.floor(offset + 0.5)
    smooth = jnp.exp(-offset * offset / (2.0 * kernel_width * kernel_width)) * amplitude[None, :]
    smooth_scale = math.sqrt((1.0 - NOISE_SHARE) / (NORB * 3.3393 * kernel_width * 1.7724539))
    noise_scale = math.sqrt(NOISE_SHARE / (NORB * 3.3393))
    noise_part = jnp.clip(jax.random.normal(noise_key, (count_of_rows, NORB), jnp.float32), -5.0, 5.0)
    row_scales = jnp.exp(jax.random.uniform(row_key, (count_of_rows, 1), jnp.float32, -0.2231, 0.2231))
    value_entries = row_scales * scales[None, :] * (smooth_scale * smooth + noise_scale * noise_part)
    return jnp.clip(value_entries, -3.0, 3.0).astype(jnp.bfloat16)


def draw_colloc(key, part):
    return collocation(key, ROWS, 11)


def draw_block_colloc(key, part):
    return collocation(key, PANEL_COLUMNS, 13)


def factor_values(key, count_of_rows, dispersion, salt_value):
    starting_key = jax.random.fold_in(key, salt_value)
    value_entries = jnp.clip(jax.random.normal(starting_key, (count_of_rows, FINISHED_COLUMNS), jnp.float32), -4.0, 4.0)
    return (dispersion * value_entries).astype(jnp.float32)


def draw_block_factor(key, part):
    dispersion = math.sqrt(0.035) / (math.sqrt(PANEL_COLUMNS) + math.sqrt(FINISHED_COLUMNS))
    return factor_values(key, PANEL_COLUMNS, dispersion, 17)


def draw_factor(key, part):
    return factor_values(key, ROWS, LOW_SCALE, 19)


def setup_inputs(seed: int = 0) -> dict:
    key_of = jax.random.split(jax.random.key(seed), 5)
    colloc = draw_colloc(jax.random.fold_in(key_of[4], 71), 0)
    block_colloc = draw_block_colloc(jax.random.fold_in(key_of[4], 71), 0)
    factor = draw_factor(jax.random.fold_in(key_of[4], 71), 0)
    block_factor = draw_block_factor(jax.random.fold_in(key_of[4], 71), 0)
    return dict(colloc=colloc, block_colloc=block_colloc, factor=factor, block_factor=block_factor)


DAMPING = 0.0625

def reference(colloc, block_colloc, factor, block_factor):
    metric_block = jnp.dot(block_colloc.astype(jnp.float32), block_colloc.T.astype(jnp.float32), preferred_element_type=jnp.float32)
    gram_low = jnp.dot(colloc.astype(jnp.float32), block_colloc.T.astype(jnp.float32), preferred_element_type=jnp.float32)
    update_block = jnp.dot(block_factor.astype(jnp.float32), block_factor.T.astype(jnp.float32), precision=lax.Precision.HIGHEST, preferred_element_type=jnp.float32)
    update_low = jnp.dot(factor.astype(jnp.float32), block_factor.T.astype(jnp.float32), precision=lax.Precision.HIGHEST, preferred_element_type=jnp.float32)
    identity = jnp.eye(PANEL_COLUMNS, dtype=jnp.float32)
    schur = metric_block * metric_block + DAMPING * identity - update_block
    cholesky_factor = jnp.linalg.cholesky(schur)
    below_rows = gram_low * gram_low - update_low
    panel_rows = lax.linalg.triangular_solve(cholesky_factor, below_rows, left_side=False, lower=True, transpose_a=True)
    return (cholesky_factor, panel_rows.reshape(BANDS, RB, PANEL_COLUMNS))
```

```python
import functools

import jax
import jax.numpy as jnp
from jax import lax
from jax.experimental import pallas as pl
from jax.experimental.pallas import tpu as pltpu
from jax.sharding import PartitionSpec as P

DAMPING = 0.0625
HI = lax.Precision.HIGHEST
MESH = pl.DeviceIdType.MESH
F32 = jnp.float32
VMEM = pl.BlockSpec(memory_space=pltpu.VMEM)


def dot(a, b, ca, cb, precision=None):
    return lax.dot_general(a, b, (((ca,), (cb,)), ((), ())), precision=precision, preferred_element_type=F32)


def place(x, y, zl, zh, c):
    return {"grp": y * 4 + zh * 2 + c, "dev": x * 8 + zl}


def exchange(bc, bf, bca, bfa, sb, xbc, xbf, part, rcore, acc, ry, s2, rz,
             zr, zs, xr, xs, br, bs, cr, cs, yr, ys, hr, hs, pr, ps, ar, as_, dr, ds, er, es):
    g = lax.axis_index("grp")
    d = lax.axis_index("dev")
    y, zh, c = g // 4, (g // 2) % 2, g % 2
    x, zl = d // 8, d % 8
    sent = []

    def push(src, dst, ssem, rsem, to, when=None):
        def make():
            return pltpu.make_async_remote_copy(
                src_ref=src(), dst_ref=dst(), send_sem=ssem, recv_sem=rsem, device_id=to(), device_id_type=MESH
            )

        if when is None:
            make().start()
        else:
            pl.when(when)(lambda: make().start())
        sent.append((when, make))

    def arrived(ref, ssem, rsem):
        pltpu.make_async_remote_copy(
            src_ref=ref, dst_ref=ref, send_sem=ssem, recv_sem=rsem,
            device_id=place(x, y, zl, zh, 1 - c), device_id_type=MESH,
        ).wait_recv()

    barrier = pltpu.get_barrier_semaphore()
    ring = [(zl + k % 8) % 8 for k in range(16)]
    half = [(zh + k // 8) % 2 for k in range(16)]
    peers = [place(x, y, zl, zh, 1 - c)]
    peers += [place(x, y, ring[k], half[k], c) for k in range(1, 16)]
    peers += [place((x + k) % 4, y, zl, zh, c) for k in range(1, 4)]
    peers += [place(x, (y + k) % 4, zl, zh, c) for k in range(1, 4)]
    for peer in peers:
        pl.semaphore_signal(barrier, inc=1, device_id=peer, device_id_type=MESH)
    pl.semaphore_wait(barrier, len(peers))

    chunks = [
        (bc, lambda slot: bca.at[slot]),
        (bf.at[0:16], lambda slot: bfa.at[slot, 0:16]),
        (bf.at[16:32], lambda slot: bfa.at[slot, 16:32]),
    ]
    for q, (own, at) in enumerate(chunks):
        for way, step in ((0, 1), (1, -1)):
            ok = (zl < 7) if step == 1 else (zl > 0)
            push(lambda own=own: own, lambda at=at: at(d), zs.at[q, 0, way], zr.at[q, zl],
                 lambda step=step: place(x, y, zl + step, zh, c), ok)
    for k in range(1, 4):
        to = lambda k=k: place((x + k) % 4, y, zl, zh, c)
        push(lambda: bc, lambda: xbc.at[x], xs.at[0, k - 1], xr.at[0, k - 1], to)
        push(lambda: bf, lambda: xbf.at[x], xs.at[1, k - 1], xr.at[1, k - 1], to)
    bca[d] = bc[...]
    bfa[d] = bf[...]
    xbc[x] = bc[...]
    xbf[x] = bf[...]
    for s in range(1, 8):
        for q, (own, at) in enumerate(chunks):
            for way, step in ((0, 1), (1, -1)):
                src = zl - step * s
                inside = (src >= 0) if step == 1 else (src <= 7)
                more = (zl < 7) if step == 1 else (zl > 0)

                @pl.when(inside)
                def _(at=at, src=src, q=q):
                    arrived(at(x * 8 + src), zs.at[q, 0, 0], zr.at[q, src])

                if s < 7:
                    push(lambda at=at, src=src: at(x * 8 + src), lambda at=at, src=src: at(x * 8 + src),
                         zs.at[q, s, way], zr.at[q, src],
                         lambda step=step: place(x, y, zl + step, zh, c), jnp.logical_and(inside, more))
    mine = pl.ds(x * 8, 8)
    for k in range(1, 4):
        to = lambda k=k: place((x + k) % 4, y, zl, zh, c)
        push(lambda: bca.at[mine], lambda: bca.at[mine], bs.at[0, k - 1], br.at[0, k - 1], to)
        push(lambda: bfa.at[mine], lambda: bfa.at[mine], bs.at[1, k - 1], br.at[1, k - 1], to)
    for k in range(1, 4):
        arrived(xbc.at[(x + 4 - k) % 4], xs.at[0, k - 1], xr.at[0, k - 1])
        arrived(xbf.at[(x + 4 - k) % 4], xs.at[1, k - 1], xr.at[1, k - 1])
    gram = dot(xbc[...].reshape(128, 500), bca[mine].reshape(256, 500), 1, 1)
    update = dot(xbf[...].reshape(128, 512), bfa[mine].reshape(256, 512), 1, 1, HI)
    for a in range(4):
        for b in range(2):
            for e in range(2):
                lo = a * 32 + b * 16 + e * 8
                part[b, a, e, 0] = gram[lo:lo + 8]
                part[b, a, e, 1] = update[lo:lo + 8]
    push(lambda: part.at[1 - c], lambda: rcore, cs, cr, lambda: place(x, y, zl, zh, 1 - c))
    arrived(rcore, cs, cr)
    acc[...] = part[c] + rcore[...]
    for k in range(1, 4):
        push(lambda k=k: acc.at[(y + k) % 4], lambda k=k: ry.at[k - 1], ys.at[k - 1], yr.at[k - 1],
             lambda k=k: place(x, (y + k) % 4, zl, zh, c))
    for k in range(1, 4):
        arrived(ry.at[k - 1], ys.at[k - 1], yr.at[k - 1])
    s2[...] = acc[y] + ry[0] + ry[1] + ry[2]
    push(lambda: s2.at[1 - zh], lambda: rz, hs, hr, lambda: place(x, y, zl, 1 - zh, c))
    arrived(rz, hs, hr)
    total = s2[zh] + rz[...]
    row = y * 256 + zl * 32 + c * 16 + zh * 8 + lax.broadcasted_iota(jnp.int32, (8, 256), 0)
    col = x * 256 + lax.broadcasted_iota(jnp.int32, (8, 256), 1)
    sb[x, y, c, zl, zh] = total[0] * total[0] + jnp.where(row == col, F32(DAMPING), F32(0.0)) - total[1]
    for k in range(1, 16):
        push(lambda: sb.at[x, y, c, zl, zh], lambda: sb.at[x, y, c, zl, zh], ps.at[k - 1], pr.at[k - 1],
             lambda k=k: place(x, y, ring[k], half[k], c))
    for k in range(1, 16):
        back_l, back_h = (zl + 8 - k % 8) % 8, (zh + k // 8) % 2
        arrived(sb.at[x, y, c, back_l, back_h], ps.at[k - 1], pr.at[k - 1])
    first = lambda k: ((x + (1 - c) * k) % 4, (y + c * k) % 4)
    second = lambda k: ((x + c * k) % 4, (y + (1 - c) * k) % 4)

    def core_copy(n, bx, by):
        push(lambda: sb.at[bx, by, c], lambda: sb.at[bx, by, c], es.at[n], er.at[n],
             lambda: place(x, y, zl, zh, 1 - c))

    for k in range(1, 4):
        push(lambda: sb.at[x, y, c], lambda: sb.at[x, y, c], as_.at[k - 1], ar.at[k - 1],
             lambda k=k: place(*first(k), zl, zh, c))
    order = []
    for m in range(4):
        bx, by = first(4 - m) if m else (x, y)
        if m:
            arrived(sb.at[bx, by, c], as_.at[m - 1], ar.at[m - 1])
        for k in range(1, 4):
            push(lambda bx=bx, by=by: sb.at[bx, by, c], lambda bx=bx, by=by: sb.at[bx, by, c],
                 ds.at[m, k - 1], dr.at[m, k - 1], lambda k=k: place(*second(k), zl, zh, c))
        core_copy(m, bx, by)
        order.append((bx, by))
    n = 4
    for k in range(1, 4):
        for m in range(4):
            bx, by = order[m]
            bx = (bx + c * (4 - k)) % 4
            by = (by + (1 - c) * (4 - k)) % 4
            arrived(sb.at[bx, by, c], ds.at[m, k - 1], dr.at[m, k - 1])
            core_copy(n, bx, by)
            order.append((bx, by))
            n += 1
    for n in range(16):
        m, k = n % 4, n // 4
        bx = (x + 8 - (c * m + (1 - c) * k)) % 4
        by = (y + 8 - ((1 - c) * m + c * k)) % 4
        arrived(sb.at[bx, by, 1 - c], es.at[n], er.at[n])
    for k in range(1, 4):
        other = pl.ds(((x + 4 - k) % 4) * 8, 8)
        arrived(bca.at[other], bs.at[0, k - 1], br.at[0, k - 1])
        arrived(bfa.at[other], bs.at[1, k - 1], br.at[1, k - 1])
    for when, make in sent:
        if when is None:
            make().wait_send()
        else:
            pl.when(when)(lambda make=make: make().wait_send())


def exchanged(bc, bf):
    D = pltpu.SemaphoreType.DMA
    return pl.pallas_call(
        exchange,
        out_shape=[
            jax.ShapeDtypeStruct((32, 32, 500), jnp.bfloat16),
            jax.ShapeDtypeStruct((32, 32, 512), F32),
            jax.ShapeDtypeStruct((4, 4, 2, 8, 2, 8, 256), F32),
        ],
        in_specs=[VMEM] * 2,
        out_specs=[VMEM] * 3,
        scratch_shapes=[
            pltpu.VMEM((4, 32, 500), jnp.bfloat16),
            pltpu.VMEM((4, 32, 512), F32),
            pltpu.VMEM((2, 4, 2, 2, 8, 256), F32),
            pltpu.VMEM((4, 2, 2, 8, 256), F32),
            pltpu.VMEM((4, 2, 2, 8, 256), F32),
            pltpu.VMEM((3, 2, 2, 8, 256), F32),
            pltpu.VMEM((2, 2, 8, 256), F32),
            pltpu.VMEM((2, 8, 256), F32),
            D((3, 8)), D((3, 7, 2)), D((2, 3)), D((2, 3)), D((2, 3)), D((2, 3)),
            D, D, D((3,)), D((3,)), D, D, D((15,)), D((15,)), D((3,)), D((3,)),
            D((4, 3)), D((4, 3)), D((16,)), D((16,)),
        ],
        compiler_params=pltpu.CompilerParams(collective_id=0, has_side_effects=True, vmem_limit_bytes=40 * 2**20),
        name="exchange",
    )(bc, bf)


def diagonal(w):
    sub = lax.broadcasted_iota(jnp.int32, (8, 128), 0)
    wide = (8, 128)
    for g in range(16):
        rows = slice(8 * g, 8 * g + 8)
        r0, r1 = w[rows, 0:128], w[rows, 128:256]
        cols = [jnp.broadcast_to(r0[:, 8 * g + k:8 * g + k + 1], wide) for k in range(8)]
        scale = jnp.zeros(wide, F32)
        for k in range(8):
            inv = lax.rsqrt(jnp.broadcast_to(cols[k][k:k + 1, :], wide))
            scale = jnp.where(sub == k, inv, scale)
            if k < 7:
                mult = jnp.where(sub > k, cols[k] * (inv * inv), 0.0)
                r0 = r0 - mult * jnp.broadcast_to(r0[k:k + 1, :], wide)
                r1 = r1 - mult * jnp.broadcast_to(r1[k:k + 1, :], wide)
                for j in range(k + 1, 8):
                    cols[j] = cols[j] - mult * jnp.broadcast_to(cols[j][k:k + 1, :], wide)
        u0, u1 = r0 * scale, r1 * scale
        w[rows, 0:128] = u0
        w[rows, 128:256] = u1
        if g < 15:
            change = dot(u0, jnp.concatenate([u0, u1], axis=1), 0, 0, HI)
            w[8 * g + 8:128, :] = w[8 * g + 8:128, :] - change[8 * g + 8:128, :]


def factorize(sb, s, t, w):
    row = lax.broadcasted_iota(jnp.int32, (128, 128), 0)
    col = lax.broadcasted_iota(jnp.int32, (128, 128), 1)
    eye = jnp.where(row == col, F32(1.0), F32(0.0))

    def load(zl, _):
        for a in range(4):
            for b in range(4):
                for c in range(2):
                    for h in range(2):
                        at = pl.multiple_of(b * 256 + zl * 32 + c * 16 + h * 8, 8)
                        s[pl.ds(at, 8), a * 256:a * 256 + 256] = sb[a, b, c, zl, h]
        return 0

    lax.fori_loop(0, 8, load, 0)

    def block(j, _):
        dj = pl.ds(pl.multiple_of(j * 128, 128), 128)
        w[:, 0:128] = s[dj, dj]
        w[:, 128:256] = eye
        diagonal(w)
        s[dj, dj] = jnp.where(col >= row, w[:, 0:128], 0.0)
        t[dj, :] = w[:, 128:256]

        def across(i, _):
            di = pl.ds(pl.multiple_of(i * 128, 128), 128)
            s[dj, di] = dot(t[dj, :], s[dj, di], 1, 0, HI)
            return 0

        lax.fori_loop(j + 1, 8, across, 0)

        def trailing(i, _):
            di = pl.ds(pl.multiple_of(i * 128, 128), 128)
            left = s[dj, di]

            def tile(k, _):
                dk = pl.ds(pl.multiple_of(k * 128, 128), 128)
                s[di, dk] = s[di, dk] - dot(left, s[dj, dk], 0, 0, HI)
                return 0

            lax.fori_loop(i, 8, tile, 0)
            return 0

        lax.fori_loop(j + 1, 8, trailing, 0)
        return 0

    lax.fori_loop(0, 8, block, 0)


def factorized(sb):
    return pl.pallas_call(
        factorize,
        out_shape=[jax.ShapeDtypeStruct((1024, 1024), F32), jax.ShapeDtypeStruct((1024, 128), F32)],
        in_specs=[VMEM],
        out_specs=[VMEM] * 2,
        scratch_shapes=[pltpu.VMEM((128, 256), F32)],
        compiler_params=pltpu.CompilerParams(vmem_limit_bytes=40 * 2**20),
        cost_estimate=pl.CostEstimate(flops=60 * 10**9, bytes_accessed=8 * 2**20, transcendentals=0),
        name="factorize",
    )(sb)


def finish(u, t, gu, lower, panel, r):
    d = lax.axis_index("dev")
    r[...] = gu[:, 0] * gu[:, 0] - gu[:, 1]
    for j in range(8):
        a, b = j * 128, j * 128 + 128
        xj = dot(r[:, a:b], t[a:b, :], 1, 1, HI)
        panel[0, :, a:b] = xj
        if j < 7:
            r[:, b:] = r[:, b:] - dot(xj, u[a:b, b:], 1, 0, HI)
    tile = pl.ds(pl.multiple_of((d // 4) * 128, 128), 128)
    for j in range(8):
        r2 = u[j * 128:j * 128 + 128, tile].T
        for q in range(4):
            @pl.when(d % 4 == q)
            def _(q=q):
                lower[:, j * 128:j * 128 + 128] = jnp.where(d // 4 >= j, r2[q * 32:q * 32 + 32, :], 0.0)


def finished(u, t, gu):
    return pl.pallas_call(
        finish,
        out_shape=[jax.ShapeDtypeStruct((32, 1024), F32), jax.ShapeDtypeStruct((1, 24, 1024), F32)],
        in_specs=[VMEM] * 3,
        out_specs=[VMEM] * 2,
        scratch_shapes=[pltpu.VMEM((24, 1024), F32)],
        compiler_params=pltpu.CompilerParams(vmem_limit_bytes=40 * 2**20),
        name="finish",
    )(u, t, gu)


def on_device(colloc, block_colloc, factor, block_factor):
    g = lax.axis_index("grp")
    y, zh, c = g // 4, (g // 2) % 2, g % 2
    bca, bfa, sb = exchanged(block_colloc, block_factor)
    u, t = factorized(sb)
    gram = dot(colloc, bca.reshape(1024, 500), 1, 1)
    update = dot(factor, bfa.reshape(1024, 512), 1, 1, HI)
    both = jnp.stack([gram.reshape(4, 2, 2, 24, 1024), update.reshape(4, 2, 2, 24, 1024)], axis=4)
    take = lambda v, i, ax: lax.dynamic_index_in_dim(v, i, ax, keepdims=False)
    every = range(16)
    v = take(both, c, 2) + lax.ppermute(take(both, 1 - c, 2), "grp", [(i, i ^ 1) for i in every])
    parts = [take(v, y, 0)]
    for k in range(1, 4):
        parts.append(lax.ppermute(take(v, (y + k) % 4, 0), "grp", [(i, (i + 4 * k) % 16) for i in every]))
    v = parts[0] + parts[1] + parts[2] + parts[3]
    v = take(v, zh, 0) + lax.ppermute(take(v, 1 - zh, 0), "grp", [(i, i ^ 2) for i in every])
    return tuple(finished(u, t, v))


def solution(mesh):
    placed = (P("dev", "grp"), P("dev", "grp"), P("dev", "grp"), P("dev", "grp"))
    return jax.shard_map(
        on_device,
        mesh=mesh,
        in_specs=placed,
        out_specs=(P("dev", None), P("dev", "grp", None)),
        check_vma=False,
    )
```

```python
import functools

import jax
import jax.numpy as jnp
from jax import lax
from jax.experimental import pallas as pl
from jax.experimental.pallas import tpu as pltpu
from jax.sharding import PartitionSpec as P

DAMPING = 0.0625
HI = lax.Precision.HIGHEST
MESH = pl.DeviceIdType.MESH
F32 = jnp.float32
VMEM = pl.BlockSpec(memory_space=pltpu.VMEM)


def dot(a, b, ca, cb, precision=None):
    return lax.dot_general(a, b, (((ca,), (cb,)), ((), ())), precision=precision, preferred_element_type=F32)


def place(x, y, zl, zh, c):
    return {"grp": y * 4 + zh * 2 + c, "dev": x * 8 + zl}


def exchange(bc, bf, bca, bfa, sb, xbc, xbf, part, rcore, acc, ry, s2, rz,
             zr, zs, xr, xs, br, bs, cr, cs, yr, ys, hr, hs, pr, ps, ar, as_, dr, ds, er, es):
    g = lax.axis_index("grp")
    d = lax.axis_index("dev")
    y, zh, c = g // 4, (g // 2) % 2, g % 2
    x, zl = d // 8, d % 8
    sent = []

    def push(src, dst, ssem, rsem, to, when=None):
        def make():
            return pltpu.make_async_remote_copy(
                src_ref=src(), dst_ref=dst(), send_sem=ssem, recv_sem=rsem, device_id=to(), device_id_type=MESH
            )

        if when is None:
            make().start()
        else:
            pl.when(when)(lambda: make().start())
        sent.append((when, make))

    def arrived(ref, ssem, rsem, when=None):
        def wait():
            pltpu.make_async_remote_copy(
                src_ref=ref, dst_ref=ref, send_sem=ssem, recv_sem=rsem,
                device_id=place(x, y, zl, zh, 1 - c), device_id_type=MESH,
            ).wait_recv()

        if when is None:
            wait()
        else:
            pl.when(when)(wait)

    barrier = pltpu.get_barrier_semaphore()
    ring = [(zl + k % 8) % 8 for k in range(16)]
    half = [(zh + k // 8) % 2 for k in range(16)]
    peers = [place(x, y, zl, zh, 1 - c)]
    peers += [place(x, y, ring[k], half[k], c) for k in range(1, 16)]
    peers += [place((x + k) % 4, y, zl, zh, c) for k in range(1, 4)]
    peers += [place(x, (y + k) % 4, zl, zh, c) for k in range(1, 4)]
    for peer in peers:
        pl.semaphore_signal(barrier, inc=1, device_id=peer, device_id_type=MESH)
    pl.semaphore_wait(barrier, len(peers))

    chunks = [
        (bc, lambda slot: bca.at[slot]),
        (bf.at[0:16], lambda slot: bfa.at[slot, 0:16]),
        (bf.at[16:32], lambda slot: bfa.at[slot, 16:32]),
    ]
    for q, (own, at) in enumerate(chunks):
        for way, step in ((0, 1), (1, -1)):
            ok = (zl < 7) if step == 1 else (zl > 0)
            push(lambda own=own: own, lambda at=at: at(d), zs.at[q, 0, way], zr.at[q, zl],
                 lambda step=step: place(x, y, zl + step, zh, c), ok)
    for k in range(1, 4):
        to = lambda k=k: place((x + k) % 4, y, zl, zh, c)
        push(lambda: bc, lambda: xbc.at[x], xs.at[0, k - 1], xr.at[0, k - 1], to)
        push(lambda: bf, lambda: xbf.at[x], xs.at[1, k - 1], xr.at[1, k - 1], to)
    bca[d] = bc[...]
    bfa[d] = bf[...]
    xbc[x] = bc[...]
    xbf[x] = bf[...]
    for s in range(1, 8):
        for q, (own, at) in enumerate(chunks):
            for way, step in ((0, 1), (1, -1)):
                src = zl - step * s
                inside = (src >= 0) if step == 1 else (src <= 7)
                more = (zl < 7) if step == 1 else (zl > 0)

                @pl.when(inside)
                def _(at=at, src=src, q=q):
                    arrived(at(x * 8 + src), zs.at[q, 0, 0], zr.at[q, src])

                if s < 7:
                    push(lambda at=at, src=src: at(x * 8 + src), lambda at=at, src=src: at(x * 8 + src),
                         zs.at[q, s, way], zr.at[q, src],
                         lambda step=step: place(x, y, zl + step, zh, c), jnp.logical_and(inside, more))
    mine = pl.ds(x * 8, 8)
    for k in range(1, 4):
        to = lambda k=k: place((x + k) % 4, y, zl, zh, c)
        push(lambda: bca.at[mine], lambda: bca.at[mine], bs.at[0, k - 1], br.at[0, k - 1], to)
        push(lambda: bfa.at[mine], lambda: bfa.at[mine], bs.at[1, k - 1], br.at[1, k - 1], to)
    for k in range(1, 4):
        arrived(xbc.at[(x + 4 - k) % 4], xs.at[0, k - 1], xr.at[0, k - 1])
        arrived(xbf.at[(x + 4 - k) % 4], xs.at[1, k - 1], xr.at[1, k - 1])
    gram = dot(xbc[...].reshape(128, 500), bca[mine].reshape(256, 500), 1, 1)
    update = dot(xbf[...].reshape(128, 512), bfa[mine].reshape(256, 512), 1, 1, HI)
    for a in range(4):
        for b in range(2):
            for e in range(2):
                lo = a * 32 + b * 16 + e * 8
                part[b, a, e, 0] = gram[lo:lo + 8]
                part[b, a, e, 1] = update[lo:lo + 8]
    push(lambda: part.at[1 - c], lambda: rcore, cs, cr, lambda: place(x, y, zl, zh, 1 - c))
    arrived(rcore, cs, cr)
    acc[...] = part[c] + rcore[...]
    for k in range(1, 4):
        push(lambda k=k: acc.at[(y + k) % 4], lambda k=k: ry.at[k - 1], ys.at[k - 1], yr.at[k - 1],
             lambda k=k: place(x, (y + k) % 4, zl, zh, c))
    for k in range(1, 4):
        arrived(ry.at[k - 1], ys.at[k - 1], yr.at[k - 1])
    s2[...] = acc[y] + ry[0] + ry[1] + ry[2]
    push(lambda: s2.at[1 - zh], lambda: rz, hs, hr, lambda: place(x, y, zl, 1 - zh, c))
    arrived(rz, hs, hr)
    total = s2[zh] + rz[...]
    row = y * 256 + zl * 32 + c * 16 + zh * 8 + lax.broadcasted_iota(jnp.int32, (8, 256), 0)
    col = x * 256 + lax.broadcasted_iota(jnp.int32, (8, 256), 1)
    sb[x, y, c, zl, zh] = total[0] * total[0] + jnp.where(row == col, F32(DAMPING), F32(0.0)) - total[1]
    for k in range(1, 16):
        push(lambda: sb.at[x, y, c, zl, zh], lambda: sb.at[x, y, c, zl, zh], ps.at[k - 1], pr.at[k - 1],
             lambda k=k: place(x, y, ring[k], half[k], c), x >= y)
    for k in range(1, 16):
        back_l, back_h = (zl + 8 - k % 8) % 8, (zh + k // 8) % 2
        arrived(sb.at[x, y, c, back_l, back_h], ps.at[k - 1], pr.at[k - 1], x >= y)
    first = lambda k: ((x + (1 - c) * k) % 4, (y + c * k) % 4)
    second = lambda k: ((x + c * k) % 4, (y + (1 - c) * k) % 4)

    def core_copy(n, bx, by):
        push(lambda: sb.at[bx, by, c], lambda: sb.at[bx, by, c], es.at[n], er.at[n],
             lambda: place(x, y, zl, zh, 1 - c), bx >= by)

    for k in range(1, 4):
        push(lambda: sb.at[x, y, c], lambda: sb.at[x, y, c], as_.at[k - 1], ar.at[k - 1],
             lambda k=k: place(*first(k), zl, zh, c), x >= y)
    order = []
    for m in range(4):
        bx, by = first(4 - m) if m else (x, y)
        if m:
            arrived(sb.at[bx, by, c], as_.at[m - 1], ar.at[m - 1], bx >= by)
        for k in range(1, 4):
            push(lambda bx=bx, by=by: sb.at[bx, by, c], lambda bx=bx, by=by: sb.at[bx, by, c],
                 ds.at[m, k - 1], dr.at[m, k - 1], lambda k=k: place(*second(k), zl, zh, c), bx >= by)
        core_copy(m, bx, by)
        order.append((bx, by))
    n = 4
    for k in range(1, 4):
        for m in range(4):
            bx, by = order[m]
            bx = (bx + c * (4 - k)) % 4
            by = (by + (1 - c) * (4 - k)) % 4
            arrived(sb.at[bx, by, c], ds.at[m, k - 1], dr.at[m, k - 1], bx >= by)
            core_copy(n, bx, by)
            order.append((bx, by))
            n += 1
    for n in range(16):
        m, k = n % 4, n // 4
        bx = (x + 8 - (c * m + (1 - c) * k)) % 4
        by = (y + 8 - ((1 - c) * m + c * k)) % 4
        arrived(sb.at[bx, by, 1 - c], es.at[n], er.at[n], bx >= by)
    for k in range(1, 4):
        other = pl.ds(((x + 4 - k) % 4) * 8, 8)
        arrived(bca.at[other], bs.at[0, k - 1], br.at[0, k - 1])
        arrived(bfa.at[other], bs.at[1, k - 1], br.at[1, k - 1])
    for when, make in sent:
        if when is None:
            make().wait_send()
        else:
            pl.when(when)(lambda make=make: make().wait_send())


def exchanged(bc, bf):
    D = pltpu.SemaphoreType.DMA
    return pl.pallas_call(
        exchange,
        out_shape=[
            jax.ShapeDtypeStruct((32, 32, 500), jnp.bfloat16),
            jax.ShapeDtypeStruct((32, 32, 512), F32),
            jax.ShapeDtypeStruct((4, 4, 2, 8, 2, 8, 256), F32),
        ],
        in_specs=[VMEM] * 2,
        out_specs=[VMEM] * 3,
        scratch_shapes=[
            pltpu.VMEM((4, 32, 500), jnp.bfloat16),
            pltpu.VMEM((4, 32, 512), F32),
            pltpu.VMEM((2, 4, 2, 2, 8, 256), F32),
            pltpu.VMEM((4, 2, 2, 8, 256), F32),
            pltpu.VMEM((4, 2, 2, 8, 256), F32),
            pltpu.VMEM((3, 2, 2, 8, 256), F32),
            pltpu.VMEM((2, 2, 8, 256), F32),
            pltpu.VMEM((2, 8, 256), F32),
            D((3, 8)), D((3, 7, 2)), D((2, 3)), D((2, 3)), D((2, 3)), D((2, 3)),
            D, D, D((3,)), D((3,)), D, D, D((15,)), D((15,)), D((3,)), D((3,)),
            D((4, 3)), D((4, 3)), D((16,)), D((16,)),
        ],
        compiler_params=pltpu.CompilerParams(collective_id=0, has_side_effects=True, vmem_limit_bytes=16 * 2**20),
        name="exchange",
    )(bc, bf)


def diagonal(w):
    wide = (8, 128)
    sub = lax.broadcasted_iota(jnp.int32, wide, 0)
    lane = lambda v, k: jnp.broadcast_to(v[:, k:k + 1], wide)
    line = lambda v, k: jnp.broadcast_to(v[k:k + 1, :], wide)
    r0, r1 = w[0:8, 0:128], w[0:8, 128:256]
    cols = [lane(r0, k) for k in range(8)]
    pivot = line(cols[0], 0)
    for g in range(16):
        lo = 8 * g
        more = g < 15
        if more:
            n0, n1 = w[lo + 8:lo + 16, 0:128], w[lo + 8:lo + 16, 128:256]
            left = [lane(n0, lo + k) for k in range(8)]
            ncols = [lane(n0, lo + 8 + k) for k in range(8)]
        scale = jnp.zeros(wide, F32)
        for k in range(8):
            inv = lax.rsqrt(pivot)
            inv2 = inv * inv
            if k < 7:
                e = line(cols[k + 1], k)
                pivot = line(cols[k + 1], k + 1) - (e * e) * inv2
            elif more:
                e = line(left[7], 0)
                pivot = line(ncols[0], 0) - (e * e) * inv2
            scale = jnp.where(sub == k, inv, scale)
            p0, p1 = line(r0, k), line(r1, k)
            if more:
                m2 = left[k] * inv2
            if k < 7:
                mult = jnp.where(sub > k, cols[k], 0.0) * inv2
                for j in range(k + 1, 8):
                    e = line(cols[j], k)
                    cols[j] = cols[j] - mult * e
                    if more:
                        left[j] = left[j] - m2 * e
                r0 = r0 - mult * p0
                r1 = r1 - mult * p1
            if more:
                for j in range(8):
                    ncols[j] = ncols[j] - m2 * line(left[k], j)
                n0 = n0 - m2 * p0
                n1 = n1 - m2 * p1
        u0, u1 = r0 * scale, r1 * scale
        w[lo:lo + 8, 0:128] = u0
        w[lo:lo + 8, 128:256] = u1
        if g < 14:
            change = dot(u0, jnp.concatenate([u0, u1], axis=1), 0, 0, HI)
            w[lo + 16:128, :] = w[lo + 16:128, :] - change[lo + 16:128, :]
        if more:
            r0, r1, cols = n0, n1, ncols


def factorize(colloc, factor, bca, bfa, sb, s, t, r, w, part, rcore, acc, ry, s2, rz, cs, cr, ys, yr, hs, hr):
    g = lax.axis_index("grp")
    d = lax.axis_index("dev")
    y, zh, c = g // 4, (g // 2) % 2, g % 2
    x, zl = d // 8, d % 8

    def core_copy():
        return pltpu.make_async_remote_copy(
            src_ref=part.at[1 - c], dst_ref=rcore, send_sem=cs, recv_sem=cr,
            device_id=place(x, y, zl, zh, 1 - c), device_id_type=MESH,
        )

    def y_copy(k):
        return pltpu.make_async_remote_copy(
            src_ref=acc.at[(y + k) % 4], dst_ref=ry.at[k - 1], send_sem=ys.at[k - 1], recv_sem=yr.at[k - 1],
            device_id=place(x, (y + k) % 4, zl, zh, c), device_id_type=MESH,
        )

    def half_copy():
        return pltpu.make_async_remote_copy(
            src_ref=s2.at[1 - zh], dst_ref=rz, send_sem=hs, recv_sem=hr,
            device_id=place(x, y, zl, 1 - zh, c), device_id_type=MESH,
        )

    barrier = pltpu.get_barrier_semaphore()
    peers = [place(x, y, zl, zh, 1 - c), place(x, y, zl, 1 - zh, c)]
    peers += [place(x, (y + k) % 4, zl, zh, c) for k in range(1, 4)]
    for peer in peers:
        pl.semaphore_signal(barrier, inc=1, device_id=peer, device_id_type=MESH)
    for b in range(4):
        rows = slice(96 * b, 96 * b + 96)
        gram = dot(colloc[rows, :], bca[...], 1, 1)
        update = dot(factor[rows, :], bfa[...], 1, 1, HI)
        for h in range(2):
            for k in range(2):
                lo = (h * 2 + k) * 24
                part[k, b, h, 0] = gram[lo:lo + 24]
                part[k, b, h, 1] = update[lo:lo + 24]
    pl.semaphore_wait(barrier, len(peers))
    core_copy().start()

    def load(i, _):
        for b in range(4):
            for k in range(2):
                for h in range(2):
                    at = pl.multiple_of(b * 256 + i * 32 + k * 16 + h * 8, 8)
                    for a in range(b, 4):
                        s[pl.ds(at, 8), a * 256:a * 256 + 256] = sb[a, b, k, i, h]
        return 0

    lax.fori_loop(0, 8, load, 0)

    row = lax.broadcasted_iota(jnp.int32, (128, 128), 0)
    col = lax.broadcasted_iota(jnp.int32, (128, 128), 1)
    eye = jnp.where(row == col, F32(1.0), F32(0.0))

    def block(j, _):
        dj = pl.ds(pl.multiple_of(j * 128, 128), 128)
        w[:, 0:128] = s[dj, dj]
        w[:, 128:256] = eye
        diagonal(w)
        t[dj, :] = w[:, 128:256]

        def across(k, _):
            dk = pl.ds(pl.multiple_of(k * 256, 256), 256)
            s[dj, dk] = dot(t[dj, :], s[dj, dk], 1, 0, HI)
            return 0

        lax.fori_loop((j + 1) // 2, 4, across, 0)
        s[dj, dj] = jnp.where(col >= row, w[:, 0:128], 0.0)

        def trailing(i, _):
            di = pl.ds(pl.multiple_of(i * 128, 128), 128)
            left = s[dj, di]

            def tile(k, _):
                dk = pl.ds(pl.multiple_of(k * 256, 256), 256)
                s[di, dk] = s[di, dk] - dot(left, s[dj, dk], 0, 0, HI)
                return 0

            lax.fori_loop(i // 2, 4, tile, 0)
            return 0

        lax.fori_loop(j + 1, 8, trailing, 0)

        @pl.when(j == 0)
        def _():
            core_copy().wait_recv()
            for b in range(4):
                acc[b] = part[c, b] + rcore[b]
            for k in range(1, 4):
                y_copy(k).start()

        @pl.when(j == 3)
        def _():
            for k in range(1, 4):
                y_copy(k).wait_recv()
            s2[...] = acc[y] + ry[0] + ry[1] + ry[2]
            half_copy().start()

        return 0

    lax.fori_loop(0, 8, block, 0)
    half_copy().wait_recv()
    gram = s2[zh, 0] + rz[0]
    r[...] = gram * gram - (s2[zh, 1] + rz[1])
    core_copy().wait_send()
    for k in range(1, 4):
        y_copy(k).wait_send()
    half_copy().wait_send()


def factorized(colloc, factor, bca, bfa, sb):
    D = pltpu.SemaphoreType.DMA
    return pl.pallas_call(
        factorize,
        out_shape=[
            jax.ShapeDtypeStruct((1024, 1024), F32),
            jax.ShapeDtypeStruct((1024, 128), F32),
            jax.ShapeDtypeStruct((24, 1024), F32),
        ],
        in_specs=[VMEM] * 5,
        out_specs=[VMEM] * 3,
        scratch_shapes=[
            pltpu.VMEM((128, 256), F32),
            pltpu.VMEM((2, 4, 2, 2, 24, 1024), F32),
            pltpu.VMEM((4, 2, 2, 24, 1024), F32),
            pltpu.VMEM((4, 2, 2, 24, 1024), F32),
            pltpu.VMEM((3, 2, 2, 24, 1024), F32),
            pltpu.VMEM((2, 2, 24, 1024), F32),
            pltpu.VMEM((2, 24, 1024), F32),
            D, D, D((3,)), D((3,)), D, D,
        ],
        compiler_params=pltpu.CompilerParams(collective_id=1, has_side_effects=True, vmem_limit_bytes=24 * 2**20),
        name="factorize",
    )(colloc, factor, bca, bfa, sb)


def finish(u, t, below, lower, panel, r):
    d = lax.axis_index("dev")
    r[...] = below[...]
    for j in range(8):
        a, b = j * 128, j * 128 + 128
        xj = dot(r[:, a:b], t[a:b, :], 1, 1, HI)
        panel[0, :, a:b] = xj
        if j < 7:
            r[:, b:] = r[:, b:] - dot(xj, u[a:b, b:], 1, 0, HI)
    tile = pl.ds(pl.multiple_of((d // 4) * 128, 128), 128)
    for j in range(8):
        r2 = u[j * 128:j * 128 + 128, tile].T
        for q in range(4):
            @pl.when(d % 4 == q)
            def _(q=q):
                lower[:, j * 128:j * 128 + 128] = jnp.where(d // 4 >= j, r2[q * 32:q * 32 + 32, :], 0.0)


def finished(u, t, below):
    return pl.pallas_call(
        finish,
        out_shape=[jax.ShapeDtypeStruct((32, 1024), F32), jax.ShapeDtypeStruct((1, 24, 1024), F32)],
        in_specs=[VMEM] * 3,
        out_specs=[VMEM] * 2,
        scratch_shapes=[pltpu.VMEM((24, 1024), F32)],
        compiler_params=pltpu.CompilerParams(vmem_limit_bytes=40 * 2**20),
        name="finish",
    )(u, t, below)


def on_device(colloc, block_colloc, factor, block_factor):
    bca, bfa, sb = exchanged(block_colloc, block_factor)
    return tuple(finished(*factorized(colloc, factor, bca.reshape(1024, 500), bfa.reshape(1024, 512), sb)))


def solution(mesh):
    placed = (P("dev", "grp"), P("dev", "grp"), P("dev", "grp"), P("dev", "grp"))
    return jax.shard_map(
        on_device,
        mesh=mesh,
        in_specs=placed,
        out_specs=(P("dev", None), P("dev", "grp", None)),
        check_vma=False,
    )
```

```python
import functools

import jax
import jax.numpy as jnp
from jax import lax
from jax.experimental import pallas as pl
from jax.experimental.pallas import tpu as pltpu
from jax.sharding import PartitionSpec as P

DAMPING = 0.0625
HI = lax.Precision.HIGHEST
MESH = pl.DeviceIdType.MESH
F32 = jnp.float32
VMEM = pl.BlockSpec(memory_space=pltpu.VMEM)


def dot(a, b, ca, cb, precision=None):
    return lax.dot_general(a, b, (((ca,), (cb,)), ((), ())), precision=precision, preferred_element_type=F32)


def place(x, y, zl, zh, c):
    return {"grp": y * 4 + zh * 2 + c, "dev": x * 8 + zl}


def exchange(colloc, bc, factor, bf, acc, sb, bca, bfa, tall, wide, part, theirs, dpart, rcore, dacc, ry, s2, rz,
             ls, zr, zs, xr, xs, cs, cr, ys, yr, hs, hr, pr, ps, ar, as_, dr, ds, gr, gs, er, es, fs, fr):
    g = lax.axis_index("grp")
    d = lax.axis_index("dev")
    y, zh, c = g // 4, (g // 2) % 2, g % 2
    x, zl = d // 8, d % 8
    sent = []

    local = [
        pltpu.make_async_copy(bc, bca.at[d], ls.at[0]),
        pltpu.make_async_copy(bf, bfa.at[d], ls.at[1]),
        pltpu.make_async_copy(colloc, tall, ls.at[2]),
        pltpu.make_async_copy(factor, wide, ls.at[3]),
    ]
    for copy in local:
        copy.start()

    def push(src, dst, ssem, rsem, to, when=None):
        def make():
            return pltpu.make_async_remote_copy(
                src_ref=src(), dst_ref=dst(), send_sem=ssem, recv_sem=rsem, device_id=to(), device_id_type=MESH
            )

        if when is None:
            make().start()
        else:
            pl.when(when)(lambda: make().start())
        sent.append((when, make))

    def arrived(ref, ssem, rsem, when=None):
        def wait():
            pltpu.make_async_remote_copy(
                src_ref=ref, dst_ref=ref, send_sem=ssem, recv_sem=rsem,
                device_id=place(x, y, zl, zh, 1 - c), device_id_type=MESH,
            ).wait_recv()

        if when is None:
            wait()
        else:
            pl.when(when)(wait)

    barrier = pltpu.get_barrier_semaphore()
    ring = [(zl + k % 8) % 8 for k in range(16)]
    half = [(zh + k // 8) % 2 for k in range(16)]
    peers = [place(x, y, zl, zh, 1 - c)]
    peers += [place(x, y, ring[k], half[k], c) for k in range(1, 16)]
    peers += [place((x + k) % 4, y, zl, zh, c) for k in range(1, 4)]
    peers += [place(x, (y + k) % 4, zl, zh, c) for k in range(1, 4)]
    for peer in peers:
        pl.semaphore_signal(barrier, inc=1, device_id=peer, device_id_type=MESH)
    pl.semaphore_wait(barrier, len(peers))

    chunks = [
        (bc, lambda slot: bca.at[slot]),
        (bf.at[0:16], lambda slot: bfa.at[slot, 0:16]),
        (bf.at[16:32], lambda slot: bfa.at[slot, 16:32]),
    ]
    whole = [(bc, lambda slot: bca.at[slot]), (bf, lambda slot: bfa.at[slot])]
    over = [lambda: place((x + 1) % 4, y, zl, zh, c), lambda: place((x + 3) % 4, y, zl, zh, c)]

    def to_x(src, own, when=None):
        for q, (mine, at) in enumerate(whole):
            for way in range(2):
                source = (lambda mine=mine: mine) if own else (lambda at=at: at(x * 8 + src))
                push(source, lambda at=at: at(x * 8 + src), xs.at[way, q, src], xr.at[way, q, src], over[way], when)

    def from_x(src):
        for q, (_, at) in enumerate(whole):
            for way in range(2):
                slot = ((x + 3 + 2 * way) % 4) * 8 + src
                arrived(at(slot), xs.at[way, q, src], xr.at[way, q, src])
                push(lambda at=at, slot=slot: at(slot), lambda at=at, slot=slot: at(slot),
                     xs.at[2, q, src], xr.at[2, q, src], over[way], (src % 2) == way)

    def from_far(src):
        for q, (_, at) in enumerate(whole):
            arrived(at(((x + 2) % 4) * 8 + src), xs.at[2, q, src], xr.at[2, q, src])

    for q, (own, at) in enumerate(chunks):
        for way, step in ((0, 1), (1, -1)):
            ok = (zl < 7) if step == 1 else (zl > 0)
            push(lambda own=own: own, lambda at=at: at(d), zs.at[q, 0, way], zr.at[q, zl],
                 lambda step=step: place(x, y, zl + step, zh, c), ok)
    to_x(zl, True)
    for s in range(1, 8):
        for q, (own, at) in enumerate(chunks):
            for way, step in ((0, 1), (1, -1)):
                src = zl - step * s
                inside = (src >= 0) if step == 1 else (src <= 7)
                more = (zl < 7) if step == 1 else (zl > 0)

                @pl.when(inside)
                def _(at=at, src=src, q=q):
                    arrived(at(x * 8 + src), zs.at[q, 0, 0], zr.at[q, src])

                if s < 7:
                    push(lambda at=at, src=src: at(x * 8 + src), lambda at=at, src=src: at(x * 8 + src),
                         zs.at[q, s, way], zr.at[q, src],
                         lambda step=step: place(x, y, zl + step, zh, c), jnp.logical_and(inside, more))
        for step in (1, -1):
            src = zl - step * s
            to_x(src, False, (src >= 0) if step == 1 else (src <= 7))
        if s == 2:
            from_x(zl)
    mine = pl.ds(x * 8, 8)
    local[0].wait()
    local[1].wait()
    from_far(zl)
    rows = [a * 8 + zl for a in range(4)]
    gram = dot(jnp.concatenate([bca[i] for i in rows], axis=0), bca[mine].reshape(256, 500), 1, 1)
    update = dot(jnp.concatenate([bfa[i] for i in rows], axis=0), bfa[mine].reshape(256, 512), 1, 1, HI)
    for a in range(4):
        for b in range(2):
            for e in range(2):
                lo = a * 32 + b * 16 + e * 8
                dpart[b, a, e, 0] = gram[lo:lo + 8]
                dpart[b, a, e, 1] = update[lo:lo + 8]
    push(lambda: dpart.at[1 - c], lambda: rcore, cs, cr, lambda: place(x, y, zl, zh, 1 - c))
    for k in range(1, 8):
        from_x((zl + k) % 8)
    arrived(rcore, cs, cr)
    dacc[...] = dpart[c] + rcore[...]
    for k in range(1, 4):
        push(lambda k=k: dacc.at[(y + k) % 4], lambda k=k: ry.at[k - 1], ys.at[k - 1], yr.at[k - 1],
             lambda k=k: place(x, (y + k) % 4, zl, zh, c))
    for k in range(1, 4):
        arrived(ry.at[k - 1], ys.at[k - 1], yr.at[k - 1])
    s2[...] = dacc[y] + ry[0] + ry[1] + ry[2]
    push(lambda: s2.at[1 - zh], lambda: rz, hs, hr, lambda: place(x, y, zl, 1 - zh, c))
    for k in range(1, 8):
        from_far((zl + k) % 8)
    local[2].wait()
    local[3].wait()
    for b in range(3):
        gram = dot(tall[:, 128 * b:128 * b + 128], bca[...].reshape(1024, 500), 0, 1)
        for n in range(16):
            lo, hi = max(24 * n, 128 * b), min(24 * n + 24, 128 * b + 128)
            if lo < hi:
                part[n % 2, n // 4, (n // 2) % 2, 0, lo - 24 * n:hi - 24 * n] = gram[lo - 128 * b:hi - 128 * b]
    for b in range(4):
        update = dot(wide[96 * b:96 * b + 96, :], bfa[...].reshape(1024, 512), 1, 1, HI)
        for h in range(2):
            for k in range(2):
                lo = (h * 2 + k) * 24
                part[k, b, h, 1] = update[lo:lo + 24]
    push(lambda: part.at[1 - c], lambda: theirs, fs, fr, lambda: place(x, y, zl, zh, 1 - c))
    arrived(rz, hs, hr)
    total = s2[zh] + rz[...]
    row = y * 256 + zl * 32 + c * 16 + zh * 8 + lax.broadcasted_iota(jnp.int32, (8, 256), 0)
    col = x * 256 + lax.broadcasted_iota(jnp.int32, (8, 256), 1)
    sb[x, y, c, zl, zh] = total[0] * total[0] + jnp.where(row == col, F32(DAMPING), F32(0.0)) - total[1]
    for k in range(1, 16):
        push(lambda: sb.at[x, y, c, zl, zh], lambda: sb.at[x, y, c, zl, zh], ps.at[k - 1], pr.at[k - 1],
             lambda k=k: place(x, y, ring[k], half[k], c), x >= y)
    for k in range(1, 16):
        back_l, back_h = (zl + 8 - k % 8) % 8, (zh + k // 8) % 2
        arrived(sb.at[x, y, c, back_l, back_h], ps.at[k - 1], pr.at[k - 1], x >= y)
    first = lambda k: ((x + (1 - c) * k) % 4, (y + c * k) % 4)
    second = lambda k: ((x + c * k) % 4, (y + (1 - c) * k) % 4)

    def core_copy(n, bx, by):
        push(lambda: sb.at[bx, by, c], lambda: sb.at[bx, by, c], es.at[n], er.at[n],
             lambda: place(x, y, zl, zh, 1 - c), bx >= by)

    for k in range(1, 4):
        push(lambda: sb.at[x, y, c], lambda: sb.at[x, y, c], as_.at[k - 1], ar.at[k - 1],
             lambda k=k: place(*first(k), zl, zh, c), x >= y)
    order = []
    beside = [lambda: place(*second(1), zl, zh, c), lambda: place(*second(3), zl, zh, c)]
    for m in range(4):
        bx, by = first(4 - m) if m else (x, y)
        if m:
            arrived(sb.at[bx, by, c], as_.at[m - 1], ar.at[m - 1], bx >= by)
        for way in range(2):
            push(lambda bx=bx, by=by: sb.at[bx, by, c], lambda bx=bx, by=by: sb.at[bx, by, c],
                 ds.at[m, way], dr.at[m, way], beside[way], bx >= by)
        core_copy(m, bx, by)
        order.append((bx, by))
    shifted = lambda m, k: ((order[m][0] + c * k) % 4, (order[m][1] + (1 - c) * k) % 4)
    for m in range(4):
        for way in range(2):
            bx, by = shifted(m, 3 - 2 * way)
            arrived(sb.at[bx, by, c], ds.at[m, way], dr.at[m, way], bx >= by)
            part_of = lambda bx=bx, by=by, way=way: sb.at[bx, by, c, way * 4:way * 4 + 4]
            push(part_of, part_of, gs.at[m, way], gr.at[m, way], beside[way], bx >= by)
            core_copy(4 + (8 * way) + m, bx, by)
    arrived(theirs, fs, fr)
    for b in range(4):
        acc[b] = part[c, b] + theirs[b]
    for m in range(4):
        bx, by = shifted(m, 2)
        for way in range(2):
            arrived(sb.at[bx, by, c, way * 4:way * 4 + 4], gs.at[m, way], gr.at[m, way], bx >= by)
        core_copy(8 + m, bx, by)
    for n in range(16):
        m, k = n % 4, n // 4
        bx = (x + 8 - (c * m + (1 - c) * k)) % 4
        by = (y + 8 - ((1 - c) * m + c * k)) % 4
        arrived(sb.at[bx, by, 1 - c], es.at[n], er.at[n], bx >= by)
    for when, make in sent:
        if when is None:
            make().wait_send()
        else:
            pl.when(when)(lambda make=make: make().wait_send())


def exchanged(colloc, bc, factor, bf):
    D = pltpu.SemaphoreType.DMA
    whole = pl.BlockSpec(memory_space=pltpu.MemorySpace.HBM)
    return pl.pallas_call(
        exchange,
        out_shape=[
            jax.ShapeDtypeStruct((4, 2, 2, 24, 1024), F32),
            jax.ShapeDtypeStruct((4, 4, 2, 8, 2, 8, 256), F32),
        ],
        in_specs=[whole] * 4,
        out_specs=[VMEM] * 2,
        scratch_shapes=[
            pltpu.VMEM((32, 32, 500), jnp.bfloat16),
            pltpu.VMEM((32, 32, 512), F32),
            pltpu.VMEM((500, 384), jnp.bfloat16),
            pltpu.VMEM((384, 512), F32),
            pltpu.VMEM((2, 4, 2, 2, 24, 1024), F32),
            pltpu.VMEM((4, 2, 2, 24, 1024), F32),
            pltpu.VMEM((2, 4, 2, 2, 8, 256), F32),
            pltpu.VMEM((4, 2, 2, 8, 256), F32),
            pltpu.VMEM((4, 2, 2, 8, 256), F32),
            pltpu.VMEM((3, 2, 2, 8, 256), F32),
            pltpu.VMEM((2, 2, 8, 256), F32),
            pltpu.VMEM((2, 8, 256), F32),
            D((4,)), D((3, 8)), D((3, 7, 2)), D((3, 2, 8)), D((3, 2, 8)),
            D, D, D((3,)), D((3,)), D, D, D((15,)), D((15,)), D((3,)), D((3,)),
            D((4, 2)), D((4, 2)), D((4, 2)), D((4, 2)), D((16,)), D((16,)), D, D,
        ],
        compiler_params=pltpu.CompilerParams(collective_id=0, has_side_effects=True, vmem_limit_bytes=30 * 2**20),
        name="exchange",
    )(colloc, bc, factor, bf)


def diagonal(w):
    wide = (8, 128)
    sub = lax.broadcasted_iota(jnp.int32, wide, 0)
    lane = lambda v, k: jnp.broadcast_to(v[:, k:k + 1], wide)
    line = lambda v, k: jnp.broadcast_to(v[k:k + 1, :], wide)
    r0, r1 = w[0:8, 0:128], w[0:8, 128:256]
    cols = [lane(r0, k) for k in range(8)]
    pivot = line(cols[0], 0)
    for g in range(16):
        lo = 8 * g
        more = g < 15
        if more:
            n0, n1 = w[lo + 8:lo + 16, 0:128], w[lo + 8:lo + 16, 128:256]
            left = [lane(n0, lo + k) for k in range(8)]
            ncols = [lane(n0, lo + 8 + k) for k in range(8)]
        scale = jnp.zeros(wide, F32)
        for k in range(8):
            inv = lax.rsqrt(pivot)
            inv2 = inv * inv
            if k < 7:
                e = line(cols[k + 1], k)
                pivot = line(cols[k + 1], k + 1) - (e * e) * inv2
            elif more:
                e = line(left[7], 0)
                pivot = line(ncols[0], 0) - (e * e) * inv2
            scale = jnp.where(sub == k, inv, scale)
            p0, p1 = line(r0, k), line(r1, k)
            if more:
                m2 = left[k] * inv2
            if k < 7:
                mult = jnp.where(sub > k, cols[k], 0.0) * inv2
                for j in range(k + 1, 8):
                    e = line(cols[j], k)
                    cols[j] = cols[j] - mult * e
                    if more:
                        left[j] = left[j] - m2 * e
                r0 = r0 - mult * p0
                r1 = r1 - mult * p1
            if more:
                for j in range(8):
                    ncols[j] = ncols[j] - m2 * line(left[k], j)
                n0 = n0 - m2 * p0
                n1 = n1 - m2 * p1
        u0, u1 = r0 * scale, r1 * scale
        w[lo:lo + 8, 0:128] = u0
        w[lo:lo + 8, 128:256] = u1
        if g < 14:
            flipped = u0.T
            q0 = [line(u0, k) for k in range(8)]
            q1 = [line(u1, k) for k in range(8)]
            for h in range(8 * g + 16, 128, 8):
                a0, a1 = w[h:h + 8, 0:128], w[h:h + 8, 128:256]
                for k in range(8):
                    m = jnp.broadcast_to(flipped[h:h + 8, k:k + 1], wide)
                    a0 = a0 - m * q0[k]
                    a1 = a1 - m * q1[k]
                w[h:h + 8, 0:128] = a0
                w[h:h + 8, 128:256] = a1
        if more:
            r0, r1, cols = n0, n1, ncols


def factorize(acc, sb, s, t, r, w, ry, s2, rz, ys, yr, hs, hr):
    g = lax.axis_index("grp")
    d = lax.axis_index("dev")
    y, zh, c = g // 4, (g // 2) % 2, g % 2
    x, zl = d // 8, d % 8

    def y_copy(k):
        return pltpu.make_async_remote_copy(
            src_ref=acc.at[(y + k) % 4], dst_ref=ry.at[k - 1], send_sem=ys.at[k - 1], recv_sem=yr.at[k - 1],
            device_id=place(x, (y + k) % 4, zl, zh, c), device_id_type=MESH,
        )

    def half_copy():
        return pltpu.make_async_remote_copy(
            src_ref=s2.at[1 - zh], dst_ref=rz, send_sem=hs, recv_sem=hr,
            device_id=place(x, y, zl, 1 - zh, c), device_id_type=MESH,
        )

    barrier = pltpu.get_barrier_semaphore()
    peers = [place(x, y, zl, 1 - zh, c)]
    peers += [place(x, (y + k) % 4, zl, zh, c) for k in range(1, 4)]
    for peer in peers:
        pl.semaphore_signal(barrier, inc=1, device_id=peer, device_id_type=MESH)

    def load(i, _):
        for b in range(4):
            for k in range(2):
                for h in range(2):
                    at = pl.multiple_of(b * 256 + i * 32 + k * 16 + h * 8, 8)
                    for a in range(b, 4):
                        s[pl.ds(at, 8), a * 256:a * 256 + 256] = sb[a, b, k, i, h]
        return 0

    lax.fori_loop(0, 8, load, 0)
    pl.semaphore_wait(barrier, len(peers))
    for k in range(1, 4):
        y_copy(k).start()

    row = lax.broadcasted_iota(jnp.int32, (128, 128), 0)
    col = lax.broadcasted_iota(jnp.int32, (128, 128), 1)
    eye = jnp.where(row == col, F32(1.0), F32(0.0))

    def block(j, _):
        dj = pl.ds(pl.multiple_of(j * 128, 128), 128)
        w[:, 0:128] = s[dj, dj]
        w[:, 128:256] = eye
        diagonal(w)
        t[dj, :] = w[:, 128:256]

        def across(k, _):
            dk = pl.ds(pl.multiple_of(k * 256, 256), 256)
            s[dj, dk] = dot(t[dj, :], s[dj, dk], 1, 0, HI)
            return 0

        lax.fori_loop((j + 1) // 2, 4, across, 0)
        s[dj, dj] = jnp.where(col >= row, w[:, 0:128], 0.0)

        def trailing(i, _):
            di = pl.ds(pl.multiple_of(i * 128, 128), 128)
            left = s[dj, di]

            def tile(k, _):
                dk = pl.ds(pl.multiple_of(k * 256, 256), 256)
                s[di, dk] = s[di, dk] - dot(left, s[dj, dk], 0, 0, HI)
                return 0

            lax.fori_loop(i // 2, 4, tile, 0)
            return 0

        lax.fori_loop(j + 1, 8, trailing, 0)

        @pl.when(j == 3)
        def _():
            for k in range(1, 4):
                y_copy(k).wait_recv()
            s2[...] = acc[y] + ry[0] + ry[1] + ry[2]
            half_copy().start()

        return 0

    lax.fori_loop(0, 8, block, 0)
    half_copy().wait_recv()
    gram = s2[zh, 0] + rz[0]
    r[...] = gram * gram - (s2[zh, 1] + rz[1])
    for k in range(1, 4):
        y_copy(k).wait_send()
    half_copy().wait_send()


def factorized(acc, sb):
    D = pltpu.SemaphoreType.DMA
    return pl.pallas_call(
        factorize,
        out_shape=[
            jax.ShapeDtypeStruct((1024, 1024), F32),
            jax.ShapeDtypeStruct((1024, 128), F32),
            jax.ShapeDtypeStruct((24, 1024), F32),
        ],
        in_specs=[VMEM] * 2,
        out_specs=[VMEM] * 3,
        scratch_shapes=[
            pltpu.VMEM((128, 256), F32),
            pltpu.VMEM((3, 2, 2, 24, 1024), F32),
            pltpu.VMEM((2, 2, 24, 1024), F32),
            pltpu.VMEM((2, 24, 1024), F32),
            D((3,)), D((3,)), D, D,
        ],
        compiler_params=pltpu.CompilerParams(collective_id=1, has_side_effects=True, vmem_limit_bytes=24 * 2**20),
        name="factorize",
    )(acc, sb)


def finish(u, t, below, lower, panel, r):
    d = lax.axis_index("dev")
    r[...] = below[...]
    for j in range(8):
        a, b = j * 128, j * 128 + 128
        xj = dot(r[:, a:b], t[a:b, :], 1, 1, HI)
        panel[0, :, a:b] = xj
        if j < 7:
            r[:, b:] = r[:, b:] - dot(xj, u[a:b, b:], 1, 0, HI)
    tile = pl.ds(pl.multiple_of((d // 4) * 128, 128), 128)
    for j in range(8):
        r2 = u[j * 128:j * 128 + 128, tile].T
        for q in range(4):
            @pl.when(d % 4 == q)
            def _(q=q):
                lower[:, j * 128:j * 128 + 128] = jnp.where(d // 4 >= j, r2[q * 32:q * 32 + 32, :], 0.0)


def finished(u, t, below):
    return pl.pallas_call(
        finish,
        out_shape=[jax.ShapeDtypeStruct((32, 1024), F32), jax.ShapeDtypeStruct((1, 24, 1024), F32)],
        in_specs=[VMEM] * 3,
        out_specs=[VMEM] * 2,
        scratch_shapes=[pltpu.VMEM((24, 1024), F32)],
        compiler_params=pltpu.CompilerParams(vmem_limit_bytes=40 * 2**20),
        name="finish",
    )(u, t, below)


def on_device(colloc, block_colloc, factor, block_factor):
    acc, sb = exchanged(colloc.T, block_colloc, factor, block_factor)
    return tuple(finished(*factorized(acc, sb)))


def solution(mesh):
    placed = (P("dev", "grp"), P("dev", "grp"), P("dev", "grp"), P("dev", "grp"))
    return jax.shard_map(
        on_device,
        mesh=mesh,
        in_specs=placed,
        out_specs=(P("dev", None), P("dev", "grp", None)),
        check_vma=False,
    )
```

```python
import functools

import jax
import jax.numpy as jnp
from jax import lax
from jax.experimental import pallas as pl
from jax.experimental.pallas import tpu as pltpu
from jax.sharding import PartitionSpec as P

DAMPING = 0.0625
HI = lax.Precision.HIGHEST
MESH = pl.DeviceIdType.MESH
F32 = jnp.float32
VMEM = pl.BlockSpec(memory_space=pltpu.VMEM)


def dot(a, b, ca, cb, precision=None):
    return lax.dot_general(a, b, (((ca,), (cb,)), ((), ())), precision=precision, preferred_element_type=F32)


def place(x, y, zl, zh, c):
    return {"grp": y * 4 + zh * 2 + c, "dev": x * 8 + zl}


def exchange(colloc, bc, factor, bf, acc, sb, bca, bfa, tall, wide, part, theirs, dpart, rcore, dacc, ry, s2, rz,
             ls, zr, zs, xr, xs, cs, cr, ys, yr, hs, hr, pr, ps, ar, as_, dr, ds, gr, gs, er, es, fs, fr):
    g = lax.axis_index("grp")
    d = lax.axis_index("dev")
    y, zh, c = g // 4, (g // 2) % 2, g % 2
    x, zl = d // 8, d % 8
    sent = []

    local = [
        pltpu.make_async_copy(bc, bca.at[d], ls.at[0]),
        pltpu.make_async_copy(bf, bfa.at[d], ls.at[1]),
        pltpu.make_async_copy(colloc, tall, ls.at[2]),
        pltpu.make_async_copy(factor, wide, ls.at[3]),
    ]
    for copy in local:
        copy.start()

    def push(src, dst, ssem, rsem, to, when=None):
        def make():
            return pltpu.make_async_remote_copy(
                src_ref=src(), dst_ref=dst(), send_sem=ssem, recv_sem=rsem, device_id=to(), device_id_type=MESH
            )

        if when is None:
            make().start()
        else:
            pl.when(when)(lambda: make().start())
        sent.append((when, make))

    def arrived(ref, ssem, rsem, when=None):
        def wait():
            pltpu.make_async_remote_copy(
                src_ref=ref, dst_ref=ref, send_sem=ssem, recv_sem=rsem,
                device_id=place(x, y, zl, zh, 1 - c), device_id_type=MESH,
            ).wait_recv()

        if when is None:
            wait()
        else:
            pl.when(when)(wait)

    barrier = pltpu.get_barrier_semaphore()
    ring = [(zl + k % 8) % 8 for k in range(16)]
    half = [(zh + k // 8) % 2 for k in range(16)]
    peers = [place(x, y, zl, zh, 1 - c)]
    peers += [place(x, y, ring[k], half[k], c) for k in range(1, 16)]
    peers += [place((x + k) % 4, y, zl, zh, c) for k in range(1, 4)]
    peers += [place(x, (y + k) % 4, zl, zh, c) for k in range(1, 4)]
    for peer in peers:
        pl.semaphore_signal(barrier, inc=1, device_id=peer, device_id_type=MESH)
    pl.semaphore_wait(barrier, len(peers))

    chunks = [
        (bc, lambda slot: bca.at[slot]),
        (bf.at[0:16], lambda slot: bfa.at[slot, 0:16]),
        (bf.at[16:32], lambda slot: bfa.at[slot, 16:32]),
    ]
    whole = [(bc, lambda slot: bca.at[slot]), (bf, lambda slot: bfa.at[slot])]
    over = [lambda: place((x + 1) % 4, y, zl, zh, c), lambda: place((x + 3) % 4, y, zl, zh, c)]

    def to_x(src, own, when=None):
        for q, (mine, at) in enumerate(whole):
            for way in range(2):
                source = (lambda mine=mine: mine) if own else (lambda at=at: at(x * 8 + src))
                push(source, lambda at=at: at(x * 8 + src), xs.at[way, q, src], xr.at[way, q, src], over[way], when)

    def from_x(src):
        for q, (_, at) in enumerate(whole):
            for way in range(2):
                slot = ((x + 3 + 2 * way) % 4) * 8 + src
                arrived(at(slot), xs.at[way, q, src], xr.at[way, q, src])
                push(lambda at=at, slot=slot: at(slot), lambda at=at, slot=slot: at(slot),
                     xs.at[2, q, src], xr.at[2, q, src], over[way], (src % 2) == way)

    def from_far(src):
        for q, (_, at) in enumerate(whole):
            arrived(at(((x + 2) % 4) * 8 + src), xs.at[2, q, src], xr.at[2, q, src])

    for q, (own, at) in enumerate(chunks):
        for way, step in ((0, 1), (1, -1)):
            ok = (zl < 7) if step == 1 else (zl > 0)
            push(lambda own=own: own, lambda at=at: at(d), zs.at[q, 0, way], zr.at[q, zl],
                 lambda step=step: place(x, y, zl + step, zh, c), ok)
    to_x(zl, True)
    for s in range(1, 8):
        for q, (own, at) in enumerate(chunks):
            for way, step in ((0, 1), (1, -1)):
                src = zl - step * s
                inside = (src >= 0) if step == 1 else (src <= 7)
                more = (zl < 7) if step == 1 else (zl > 0)

                @pl.when(inside)
                def _(at=at, src=src, q=q):
                    arrived(at(x * 8 + src), zs.at[q, 0, 0], zr.at[q, src])

                if s < 7:
                    push(lambda at=at, src=src: at(x * 8 + src), lambda at=at, src=src: at(x * 8 + src),
                         zs.at[q, s, way], zr.at[q, src],
                         lambda step=step: place(x, y, zl + step, zh, c), jnp.logical_and(inside, more))
        for step in (1, -1):
            src = zl - step * s
            to_x(src, False, (src >= 0) if step == 1 else (src <= 7))
        if s == 2:
            from_x(zl)
    mine = pl.ds(x * 8, 8)
    local[0].wait()
    local[1].wait()
    from_far(zl)
    rows = [a * 8 + zl for a in range(4)]
    gram = dot(jnp.concatenate([bca[i] for i in rows], axis=0), bca[mine].reshape(256, 500), 1, 1)
    update = dot(jnp.concatenate([bfa[i] for i in rows], axis=0), bfa[mine].reshape(256, 512), 1, 1, HI)
    for a in range(4):
        for b in range(2):
            for e in range(2):
                lo = a * 32 + b * 16 + e * 8
                dpart[b, a, e, 0] = gram[lo:lo + 8]
                dpart[b, a, e, 1] = update[lo:lo + 8]
    push(lambda: dpart.at[1 - c], lambda: rcore, cs, cr, lambda: place(x, y, zl, zh, 1 - c))
    for k in range(1, 8):
        from_x((zl + k) % 8)
    arrived(rcore, cs, cr)
    dacc[...] = dpart[c] + rcore[...]
    for k in range(1, 4):
        push(lambda k=k: dacc.at[(y + k) % 4], lambda k=k: ry.at[k - 1], ys.at[k - 1], yr.at[k - 1],
             lambda k=k: place(x, (y + k) % 4, zl, zh, c))
    for k in range(1, 4):
        arrived(ry.at[k - 1], ys.at[k - 1], yr.at[k - 1])
    s2[...] = dacc[y] + ry[0] + ry[1] + ry[2]
    push(lambda: s2.at[1 - zh], lambda: rz, hs, hr, lambda: place(x, y, zl, 1 - zh, c))
    for k in range(1, 8):
        from_far((zl + k) % 8)
    local[2].wait()
    local[3].wait()
    for b in range(3):
        gram = dot(tall[:, 128 * b:128 * b + 128], bca[...].reshape(1024, 500), 0, 1)
        for n in range(16):
            lo, hi = max(24 * n, 128 * b), min(24 * n + 24, 128 * b + 128)
            if lo < hi:
                part[n % 2, n // 4, (n // 2) % 2, 0, lo - 24 * n:hi - 24 * n] = gram[lo - 128 * b:hi - 128 * b]
    for b in range(4):
        update = dot(wide[96 * b:96 * b + 96, :], bfa[...].reshape(1024, 512), 1, 1, HI)
        for h in range(2):
            for k in range(2):
                lo = (h * 2 + k) * 24
                part[k, b, h, 1] = update[lo:lo + 24]
    push(lambda: part.at[1 - c], lambda: theirs, fs, fr, lambda: place(x, y, zl, zh, 1 - c))
    arrived(rz, hs, hr)
    total = s2[zh] + rz[...]
    row = y * 256 + zl * 32 + c * 16 + zh * 8 + lax.broadcasted_iota(jnp.int32, (8, 256), 0)
    col = x * 256 + lax.broadcasted_iota(jnp.int32, (8, 256), 1)
    sb[x, y, c, zl, zh] = total[0] * total[0] + jnp.where(row == col, F32(DAMPING), F32(0.0)) - total[1]
    for k in range(1, 16):
        push(lambda: sb.at[x, y, c, zl, zh], lambda: sb.at[x, y, c, zl, zh], ps.at[k - 1], pr.at[k - 1],
             lambda k=k: place(x, y, ring[k], half[k], c), x >= y)
    for k in range(1, 16):
        back_l, back_h = (zl + 8 - k % 8) % 8, (zh + k // 8) % 2
        arrived(sb.at[x, y, c, back_l, back_h], ps.at[k - 1], pr.at[k - 1], x >= y)
    first = lambda k: ((x + (1 - c) * k) % 4, (y + c * k) % 4)
    second = lambda k: ((x + c * k) % 4, (y + (1 - c) * k) % 4)

    def core_copy(n, bx, by):
        push(lambda: sb.at[bx, by, c], lambda: sb.at[bx, by, c], es.at[n], er.at[n],
             lambda: place(x, y, zl, zh, 1 - c), bx >= by)

    for k in range(1, 4):
        push(lambda: sb.at[x, y, c], lambda: sb.at[x, y, c], as_.at[k - 1], ar.at[k - 1],
             lambda k=k: place(*first(k), zl, zh, c), x >= y)
    order = []
    beside = [lambda: place(*second(1), zl, zh, c), lambda: place(*second(3), zl, zh, c)]
    for m in range(4):
        bx, by = first(4 - m) if m else (x, y)
        if m:
            arrived(sb.at[bx, by, c], as_.at[m - 1], ar.at[m - 1], bx >= by)
        for way in range(2):
            push(lambda bx=bx, by=by: sb.at[bx, by, c], lambda bx=bx, by=by: sb.at[bx, by, c],
                 ds.at[m, way], dr.at[m, way], beside[way], bx >= by)
        core_copy(m, bx, by)
        order.append((bx, by))
    shifted = lambda m, k: ((order[m][0] + c * k) % 4, (order[m][1] + (1 - c) * k) % 4)
    for m in range(4):
        for way in range(2):
            bx, by = shifted(m, 3 - 2 * way)
            arrived(sb.at[bx, by, c], ds.at[m, way], dr.at[m, way], bx >= by)
            part_of = lambda bx=bx, by=by, way=way: sb.at[bx, by, c, way * 4:way * 4 + 4]
            push(part_of, part_of, gs.at[m, way], gr.at[m, way], beside[way], bx >= by)
            core_copy(4 + (8 * way) + m, bx, by)
    arrived(theirs, fs, fr)
    for b in range(4):
        acc[b] = part[c, b] + theirs[b]
    for m in range(4):
        bx, by = shifted(m, 2)
        for way in range(2):
            arrived(sb.at[bx, by, c, way * 4:way * 4 + 4], gs.at[m, way], gr.at[m, way], bx >= by)
        core_copy(8 + m, bx, by)
    for n in range(16):
        m, k = n % 4, n // 4
        bx = (x + 8 - (c * m + (1 - c) * k)) % 4
        by = (y + 8 - ((1 - c) * m + c * k)) % 4
        arrived(sb.at[bx, by, 1 - c], es.at[n], er.at[n], bx >= by)
    for when, make in sent:
        if when is None:
            make().wait_send()
        else:
            pl.when(when)(lambda make=make: make().wait_send())


def exchanged(colloc, bc, factor, bf):
    D = pltpu.SemaphoreType.DMA
    whole = pl.BlockSpec(memory_space=pltpu.MemorySpace.HBM)
    return pl.pallas_call(
        exchange,
        out_shape=[
            jax.ShapeDtypeStruct((4, 2, 2, 24, 1024), F32),
            jax.ShapeDtypeStruct((4, 4, 2, 8, 2, 8, 256), F32),
        ],
        in_specs=[whole] * 4,
        out_specs=[VMEM] * 2,
        scratch_shapes=[
            pltpu.VMEM((32, 32, 500), jnp.bfloat16),
            pltpu.VMEM((32, 32, 512), F32),
            pltpu.VMEM((500, 384), jnp.bfloat16),
            pltpu.VMEM((384, 512), F32),
            pltpu.VMEM((2, 4, 2, 2, 24, 1024), F32),
            pltpu.VMEM((4, 2, 2, 24, 1024), F32),
            pltpu.VMEM((2, 4, 2, 2, 8, 256), F32),
            pltpu.VMEM((4, 2, 2, 8, 256), F32),
            pltpu.VMEM((4, 2, 2, 8, 256), F32),
            pltpu.VMEM((3, 2, 2, 8, 256), F32),
            pltpu.VMEM((2, 2, 8, 256), F32),
            pltpu.VMEM((2, 8, 256), F32),
            D((4,)), D((3, 8)), D((3, 7, 2)), D((3, 2, 8)), D((3, 2, 8)),
            D, D, D((3,)), D((3,)), D, D, D((15,)), D((15,)), D((3,)), D((3,)),
            D((4, 2)), D((4, 2)), D((4, 2)), D((4, 2)), D((16,)), D((16,)), D, D,
        ],
        compiler_params=pltpu.CompilerParams(collective_id=0, has_side_effects=True, vmem_limit_bytes=30 * 2**20),
        name="exchange",
    )(colloc, bc, factor, bf)


def diagonal(w):
    wide = (8, 128)
    sub = lax.broadcasted_iota(jnp.int32, wide, 0)
    lane = lambda v, k: jnp.broadcast_to(v[:, k:k + 1], wide)
    line = lambda v, k: jnp.broadcast_to(v[k:k + 1, :], wide)
    r0, r1 = w[0:8, 0:128], w[0:8, 128:256]
    cols = [lane(r0, k) for k in range(8)]
    pivot = line(cols[0], 0)
    for g in range(16):
        lo = 8 * g
        more = g < 15
        if more:
            n0, n1 = w[lo + 8:lo + 16, 0:128], w[lo + 8:lo + 16, 128:256]
            left = [lane(n0, lo + k) for k in range(8)]
            ncols = [lane(n0, lo + 8 + k) for k in range(8)]
        scale = jnp.zeros(wide, F32)
        for k in range(8):
            inv = lax.rsqrt(pivot)
            inv2 = inv * inv
            if k < 7:
                e = line(cols[k + 1], k)
                pivot = line(cols[k + 1], k + 1) - (e * e) * inv2
            elif more:
                e = line(left[7], 0)
                pivot = line(ncols[0], 0) - (e * e) * inv2
            scale = jnp.where(sub == k, inv, scale)
            p0, p1 = line(r0, k), line(r1, k)
            if more:
                m2 = left[k] * inv2
            if k < 7:
                mult = jnp.where(sub > k, cols[k], 0.0) * inv2
                for j in range(k + 1, 8):
                    e = line(cols[j], k)
                    cols[j] = cols[j] - mult * e
                    if more:
                        left[j] = left[j] - m2 * e
                r0 = r0 - mult * p0
                r1 = r1 - mult * p1
            if more:
                for j in range(8):
                    ncols[j] = ncols[j] - m2 * line(left[k], j)
                n0 = n0 - m2 * p0
                n1 = n1 - m2 * p1
        u0, u1 = r0 * scale, r1 * scale
        w[lo:lo + 8, 0:128] = u0
        w[lo:lo + 8, 128:256] = u1
        first = g // 4 * 4
        reach = min(16, first + 6)
        if g + 2 < reach:
            flipped = u0.T
            q0 = [line(u0, k) for k in range(8)]
            q1 = [line(u1, k) for k in range(8)]
            for h in range(8 * g + 16, 8 * reach, 8):
                a0, a1 = w[h:h + 8, 0:128], w[h:h + 8, 128:256]
                for k in range(8):
                    m = jnp.broadcast_to(flipped[h:h + 8, k:k + 1], wide)
                    a0 = a0 - m * q0[k]
                    a1 = a1 - m * q1[k]
                w[h:h + 8, 0:128] = a0
                w[h:h + 8, 128:256] = a1
        if g == first + 3 and reach < 16:
            panel = w[8 * first:8 * first + 32, :]
            change = dot(panel[:, 0:128], panel, 0, 0, HI)
            w[8 * reach:128, :] = w[8 * reach:128, :] - change[8 * reach:128, :]
        if more:
            r0, r1, cols = n0, n1, ncols


def factorize(acc, sb, s, t, r, w, ry, s2, rz, ys, yr, hs, hr):
    g = lax.axis_index("grp")
    d = lax.axis_index("dev")
    y, zh, c = g // 4, (g // 2) % 2, g % 2
    x, zl = d // 8, d % 8

    def y_copy(k):
        return pltpu.make_async_remote_copy(
            src_ref=acc.at[(y + k) % 4], dst_ref=ry.at[k - 1], send_sem=ys.at[k - 1], recv_sem=yr.at[k - 1],
            device_id=place(x, (y + k) % 4, zl, zh, c), device_id_type=MESH,
        )

    def half_copy():
        return pltpu.make_async_remote_copy(
            src_ref=s2.at[1 - zh], dst_ref=rz, send_sem=hs, recv_sem=hr,
            device_id=place(x, y, zl, 1 - zh, c), device_id_type=MESH,
        )

    barrier = pltpu.get_barrier_semaphore()
    peers = [place(x, y, zl, 1 - zh, c)]
    peers += [place(x, (y + k) % 4, zl, zh, c) for k in range(1, 4)]
    for peer in peers:
        pl.semaphore_signal(barrier, inc=1, device_id=peer, device_id_type=MESH)

    def load(i, _):
        for b in range(4):
            for k in range(2):
                for h in range(2):
                    at = pl.multiple_of(b * 256 + i * 32 + k * 16 + h * 8, 8)
                    for a in range(b, 4):
                        s[pl.ds(at, 8), a * 256:a * 256 + 256] = sb[a, b, k, i, h]
        return 0

    lax.fori_loop(0, 8, load, 0)
    pl.semaphore_wait(barrier, len(peers))
    for k in range(1, 4):
        y_copy(k).start()

    row = lax.broadcasted_iota(jnp.int32, (128, 128), 0)
    col = lax.broadcasted_iota(jnp.int32, (128, 128), 1)
    eye = jnp.where(row == col, F32(1.0), F32(0.0))

    def block(j, _):
        dj = pl.ds(pl.multiple_of(j * 128, 128), 128)
        w[:, 0:128] = s[dj, dj]
        w[:, 128:256] = eye
        diagonal(w)
        t[dj, :] = w[:, 128:256]

        def across(k, _):
            dk = pl.ds(pl.multiple_of(k * 256, 256), 256)
            s[dj, dk] = dot(t[dj, :], s[dj, dk], 1, 0, HI)
            return 0

        lax.fori_loop((j + 1) // 2, 4, across, 0)
        s[dj, dj] = jnp.where(col >= row, w[:, 0:128], 0.0)

        def update(rows, start):
            left = s[dj, rows]

            def tile(k, _):
                dk = pl.ds(pl.multiple_of(k * 256, 256), 256)
                s[rows, dk] = s[rows, dk] - dot(left, s[dj, dk], 0, 0, HI)
                return 0

            lax.fori_loop(start, 4, tile, 0)

        @pl.when(j % 2 == 0)
        def _():
            update(pl.ds(pl.multiple_of(jnp.minimum(j + 1, 7) * 128, 128), 128), j // 2)

        def trailing(i, _):
            update(pl.ds(pl.multiple_of(i * 256, 256), 256), i)
            return 0

        lax.fori_loop(j // 2 + 1, 4, trailing, 0)

        @pl.when(j == 3)
        def _():
            for k in range(1, 4):
                y_copy(k).wait_recv()
            s2[...] = acc[y] + ry[0] + ry[1] + ry[2]
            half_copy().start()

        return 0

    lax.fori_loop(0, 8, block, 0)
    half_copy().wait_recv()
    gram = s2[zh, 0] + rz[0]
    r[...] = gram * gram - (s2[zh, 1] + rz[1])
    for k in range(1, 4):
        y_copy(k).wait_send()
    half_copy().wait_send()


def factorized(acc, sb):
    D = pltpu.SemaphoreType.DMA
    return pl.pallas_call(
        factorize,
        out_shape=[
            jax.ShapeDtypeStruct((1024, 1024), F32),
            jax.ShapeDtypeStruct((1024, 128), F32),
            jax.ShapeDtypeStruct((24, 1024), F32),
        ],
        in_specs=[VMEM] * 2,
        out_specs=[VMEM] * 3,
        scratch_shapes=[
            pltpu.VMEM((128, 256), F32),
            pltpu.VMEM((3, 2, 2, 24, 1024), F32),
            pltpu.VMEM((2, 2, 24, 1024), F32),
            pltpu.VMEM((2, 24, 1024), F32),
            D((3,)), D((3,)), D, D,
        ],
        compiler_params=pltpu.CompilerParams(collective_id=1, has_side_effects=True, vmem_limit_bytes=24 * 2**20),
        name="factorize",
    )(acc, sb)


def finish(u, t, below, lower, panel, r):
    d = lax.axis_index("dev")
    r[...] = below[...]
    for j in range(8):
        a, b = j * 128, j * 128 + 128
        xj = dot(r[:, a:b], t[a:b, :], 1, 1, HI)
        panel[0, :, a:b] = xj
        if j < 7:
            r[:, b:] = r[:, b:] - dot(xj, u[a:b, b:], 1, 0, HI)
    tile = pl.ds(pl.multiple_of((d // 4) * 128, 128), 128)
    for j in range(8):
        r2 = u[j * 128:j * 128 + 128, tile].T
        for q in range(4):
            @pl.when(d % 4 == q)
            def _(q=q):
                lower[:, j * 128:j * 128 + 128] = jnp.where(d // 4 >= j, r2[q * 32:q * 32 + 32, :], 0.0)


def finished(u, t, below):
    return pl.pallas_call(
        finish,
        out_shape=[jax.ShapeDtypeStruct((32, 1024), F32), jax.ShapeDtypeStruct((1, 24, 1024), F32)],
        in_specs=[VMEM] * 3,
        out_specs=[VMEM] * 2,
        scratch_shapes=[pltpu.VMEM((24, 1024), F32)],
        compiler_params=pltpu.CompilerParams(vmem_limit_bytes=40 * 2**20),
        name="finish",
    )(u, t, below)


def on_device(colloc, block_colloc, factor, block_factor):
    acc, sb = exchanged(colloc.T, block_colloc, factor, block_factor)
    return tuple(finished(*factorized(acc, sb)))


def solution(mesh):
    placed = (P("dev", "grp"), P("dev", "grp"), P("dev", "grp"), P("dev", "grp"))
    return jax.shard_map(
        on_device,
        mesh=mesh,
        in_specs=placed,
        out_specs=(P("dev", None), P("dev", "grp", None)),
        check_vma=False,
    )
```

```python
import functools

import jax
import jax.numpy as jnp
from jax import lax
from jax.experimental import pallas as pl
from jax.experimental.pallas import tpu as pltpu
from jax.sharding import PartitionSpec as P

DAMPING = 0.0625
HI = lax.Precision.HIGHEST
MESH = pl.DeviceIdType.MESH
F32 = jnp.float32
VMEM = pl.BlockSpec(memory_space=pltpu.VMEM)


def dot(a, b, ca, cb, precision=None):
    return lax.dot_general(a, b, (((ca,), (cb,)), ((), ())), precision=precision, preferred_element_type=F32)


def place(x, y, zl, zh, c):
    return {"grp": y * 4 + zh * 2 + c, "dev": x * 8 + zl}


def diagonal(w):
    wide = (8, 128)
    sub = lax.broadcasted_iota(jnp.int32, wide, 0)
    lane = lambda v, k: jnp.broadcast_to(v[:, k:k + 1], wide)
    line = lambda v, k: jnp.broadcast_to(v[k:k + 1, :], wide)
    r0, r1 = w[0:8, 0:128], w[0:8, 128:256]
    cols = [lane(r0, k) for k in range(8)]
    pivot = line(cols[0], 0)
    for g in range(16):
        lo = 8 * g
        more = g < 15
        if more:
            n0, n1 = w[lo + 8:lo + 16, 0:128], w[lo + 8:lo + 16, 128:256]
            left = [lane(n0, lo + k) for k in range(8)]
            ncols = [lane(n0, lo + 8 + k) for k in range(8)]
        scale = jnp.zeros(wide, F32)
        for k in range(8):
            inv = lax.rsqrt(pivot)
            inv2 = inv * inv
            if k < 7:
                e = line(cols[k + 1], k)
                pivot = line(cols[k + 1], k + 1) - (e * e) * inv2
            elif more:
                e = line(left[7], 0)
                pivot = line(ncols[0], 0) - (e * e) * inv2
            scale = jnp.where(sub == k, inv, scale)
            p0, p1 = line(r0, k), line(r1, k)
            if more:
                m2 = left[k] * inv2
            if k < 7:
                mult = jnp.where(sub > k, cols[k], 0.0) * inv2
                for j in range(k + 1, 8):
                    e = line(cols[j], k)
                    cols[j] = cols[j] - mult * e
                    if more:
                        left[j] = left[j] - m2 * e
                r0 = r0 - mult * p0
                r1 = r1 - mult * p1
            if more:
                for j in range(8):
                    ncols[j] = ncols[j] - m2 * line(left[k], j)
                n0 = n0 - m2 * p0
                n1 = n1 - m2 * p1
        u0, u1 = r0 * scale, r1 * scale
        w[lo:lo + 8, 0:128] = u0
        w[lo:lo + 8, 128:256] = u1
        first = g // 4 * 4
        reach = min(16, first + 6)
        if g + 2 < reach:
            flipped = u0.T
            q0 = [line(u0, k) for k in range(8)]
            q1 = [line(u1, k) for k in range(8)]
            for h in range(8 * g + 16, 8 * reach, 8):
                a0, a1 = w[h:h + 8, 0:128], w[h:h + 8, 128:256]
                for k in range(8):
                    m = jnp.broadcast_to(flipped[h:h + 8, k:k + 1], wide)
                    a0 = a0 - m * q0[k]
                    a1 = a1 - m * q1[k]
                w[h:h + 8, 0:128] = a0
                w[h:h + 8, 128:256] = a1
        if g == first + 3 and reach < 16:
            panel = w[8 * first:8 * first + 32, :]
            change = dot(panel[:, 0:128], panel, 0, 0, HI)
            w[8 * reach:128, :] = w[8 * reach:128, :] - change[8 * reach:128, :]
        if more:
            r0, r1, cols = n0, n1, ncols


def panel_step(colloc, bc, factor, bf, lower, panel, acc, sb, s, t, w, r, bca, bfa, tall, wide, part, theirs,
               dpart, rcore, dacc, ry, s2, rz, lry, ls2, lrz,
               ls, zr, zs, xr, xs, cs, cr, ys, yr, hs, hr, pr, ps, ar, as_, dr, ds, gr, gs, er, es, fs, fr,
               lys, lyr, lhs, lhr):
    g = lax.axis_index("grp")
    d = lax.axis_index("dev")
    y, zh, c = g // 4, (g // 2) % 2, g % 2
    x, zl = d // 8, d % 8
    sent = []

    local = [
        pltpu.make_async_copy(bc, bca.at[d], ls.at[0]),
        pltpu.make_async_copy(bf, bfa.at[d], ls.at[1]),
        pltpu.make_async_copy(colloc, tall, ls.at[2]),
        pltpu.make_async_copy(factor, wide, ls.at[3]),
    ]
    for copy in local:
        copy.start()

    def push(src, dst, ssem, rsem, to, when=None):
        def make():
            return pltpu.make_async_remote_copy(
                src_ref=src(), dst_ref=dst(), send_sem=ssem, recv_sem=rsem, device_id=to(), device_id_type=MESH
            )

        if when is None:
            make().start()
        else:
            pl.when(when)(lambda: make().start())
        sent.append((when, make))

    def arrived(ref, ssem, rsem, when=None):
        def wait():
            pltpu.make_async_remote_copy(
                src_ref=ref, dst_ref=ref, send_sem=ssem, recv_sem=rsem,
                device_id=place(x, y, zl, zh, 1 - c), device_id_type=MESH,
            ).wait_recv()

        if when is None:
            wait()
        else:
            pl.when(when)(wait)

    barrier = pltpu.get_barrier_semaphore()
    ring = [(zl + k % 8) % 8 for k in range(16)]
    half = [(zh + k // 8) % 2 for k in range(16)]
    peers = [place(x, y, zl, zh, 1 - c)]
    peers += [place(x, y, ring[k], half[k], c) for k in range(1, 16)]
    peers += [place((x + k) % 4, y, zl, zh, c) for k in range(1, 4)]
    peers += [place(x, (y + k) % 4, zl, zh, c) for k in range(1, 4)]
    for peer in peers:
        pl.semaphore_signal(barrier, inc=1, device_id=peer, device_id_type=MESH)
    pl.semaphore_wait(barrier, len(peers))

    chunks = [
        (bc, lambda slot: bca.at[slot]),
        (bf.at[0:16], lambda slot: bfa.at[slot, 0:16]),
        (bf.at[16:32], lambda slot: bfa.at[slot, 16:32]),
    ]
    whole = [(bc, lambda slot: bca.at[slot]), (bf, lambda slot: bfa.at[slot])]
    over = [lambda: place((x + 1) % 4, y, zl, zh, c), lambda: place((x + 3) % 4, y, zl, zh, c)]

    def to_x(src, own, when=None):
        for q, (mine, at) in enumerate(whole):
            for way in range(2):
                source = (lambda mine=mine: mine) if own else (lambda at=at: at(x * 8 + src))
                push(source, lambda at=at: at(x * 8 + src), xs.at[way, q, src], xr.at[way, q, src], over[way], when)

    def from_x(src):
        for q, (_, at) in enumerate(whole):
            for way in range(2):
                slot = ((x + 3 + 2 * way) % 4) * 8 + src
                arrived(at(slot), xs.at[way, q, src], xr.at[way, q, src])
                push(lambda at=at, slot=slot: at(slot), lambda at=at, slot=slot: at(slot),
                     xs.at[2, q, src], xr.at[2, q, src], over[way], (src % 2) == way)

    def from_far(src):
        for q, (_, at) in enumerate(whole):
            arrived(at(((x + 2) % 4) * 8 + src), xs.at[2, q, src], xr.at[2, q, src])

    for q, (own, at) in enumerate(chunks):
        for way, step in ((0, 1), (1, -1)):
            ok = (zl < 7) if step == 1 else (zl > 0)
            push(lambda own=own: own, lambda at=at: at(d), zs.at[q, 0, way], zr.at[q, zl],
                 lambda step=step: place(x, y, zl + step, zh, c), ok)
    to_x(zl, True)
    for hop in range(1, 8):
        for q, (own, at) in enumerate(chunks):
            for way, step in ((0, 1), (1, -1)):
                src = zl - step * hop
                inside = (src >= 0) if step == 1 else (src <= 7)
                more = (zl < 7) if step == 1 else (zl > 0)

                @pl.when(inside)
                def _(at=at, src=src, q=q):
                    arrived(at(x * 8 + src), zs.at[q, 0, 0], zr.at[q, src])

                if hop < 7:
                    push(lambda at=at, src=src: at(x * 8 + src), lambda at=at, src=src: at(x * 8 + src),
                         zs.at[q, hop, way], zr.at[q, src],
                         lambda step=step: place(x, y, zl + step, zh, c), jnp.logical_and(inside, more))
        for step in (1, -1):
            src = zl - step * hop
            to_x(src, False, (src >= 0) if step == 1 else (src <= 7))
        if hop == 2:
            from_x(zl)
    mine = pl.ds(x * 8, 8)
    local[0].wait()
    local[1].wait()
    from_far(zl)
    rows = [a * 8 + zl for a in range(4)]
    gram = dot(jnp.concatenate([bca[i] for i in rows], axis=0), bca[mine].reshape(256, 500), 1, 1)
    update = dot(jnp.concatenate([bfa[i] for i in rows], axis=0), bfa[mine].reshape(256, 512), 1, 1, HI)
    for a in range(4):
        for b in range(2):
            for e in range(2):
                lo = a * 32 + b * 16 + e * 8
                dpart[b, a, e, 0] = gram[lo:lo + 8]
                dpart[b, a, e, 1] = update[lo:lo + 8]
    push(lambda: dpart.at[1 - c], lambda: rcore, cs, cr, lambda: place(x, y, zl, zh, 1 - c))
    for k in range(1, 8):
        from_x((zl + k) % 8)
    arrived(rcore, cs, cr)
    dacc[...] = dpart[c] + rcore[...]
    for k in range(1, 4):
        push(lambda k=k: dacc.at[(y + k) % 4], lambda k=k: ry.at[k - 1], ys.at[k - 1], yr.at[k - 1],
             lambda k=k: place(x, (y + k) % 4, zl, zh, c))
    for k in range(1, 4):
        arrived(ry.at[k - 1], ys.at[k - 1], yr.at[k - 1])
    s2[...] = dacc[y] + ry[0] + ry[1] + ry[2]
    push(lambda: s2.at[1 - zh], lambda: rz, hs, hr, lambda: place(x, y, zl, 1 - zh, c))
    for k in range(1, 8):
        from_far((zl + k) % 8)
    local[2].wait()
    local[3].wait()
    for b in range(3):
        gram = dot(tall[:, 128 * b:128 * b + 128], bca[...].reshape(1024, 500), 0, 1)
        for n in range(16):
            lo, hi = max(24 * n, 128 * b), min(24 * n + 24, 128 * b + 128)
            if lo < hi:
                part[n % 2, n // 4, (n // 2) % 2, 0, lo - 24 * n:hi - 24 * n] = gram[lo - 128 * b:hi - 128 * b]

    def products(b):
        update = dot(wide[96 * b:96 * b + 96, :], bfa[...].reshape(1024, 512), 1, 1, HI)
        for h in range(2):
            for k in range(2):
                lo = (h * 2 + k) * 24
                part[k, b, h, 1] = update[lo:lo + 24]

    products(0)
    products(1)
    arrived(rz, hs, hr)
    total = s2[zh] + rz[...]
    row = y * 256 + zl * 32 + c * 16 + zh * 8 + lax.broadcasted_iota(jnp.int32, (8, 256), 0)
    col = x * 256 + lax.broadcasted_iota(jnp.int32, (8, 256), 1)
    sb[x, y, c, zl, zh] = total[0] * total[0] + jnp.where(row == col, F32(DAMPING), F32(0.0)) - total[1]
    for k in range(1, 16):
        push(lambda: sb.at[x, y, c, zl, zh], lambda: sb.at[x, y, c, zl, zh], ps.at[k - 1], pr.at[k - 1],
             lambda k=k: place(x, y, ring[k], half[k], c), x >= y)
    products(2)
    products(3)
    push(lambda: part.at[1 - c], lambda: theirs, fs, fr, lambda: place(x, y, zl, zh, 1 - c))
    for k in range(1, 16):
        back_l, back_h = (zl + 8 - k % 8) % 8, (zh + k // 8) % 2
        arrived(sb.at[x, y, c, back_l, back_h], ps.at[k - 1], pr.at[k - 1], x >= y)
    first = lambda k: ((x + (1 - c) * k) % 4, (y + c * k) % 4)
    second = lambda k: ((x + c * k) % 4, (y + (1 - c) * k) % 4)

    def core_copy(n, bx, by):
        push(lambda: sb.at[bx, by, c], lambda: sb.at[bx, by, c], es.at[n], er.at[n],
             lambda: place(x, y, zl, zh, 1 - c), bx >= by)

    for k in range(1, 4):
        push(lambda: sb.at[x, y, c], lambda: sb.at[x, y, c], as_.at[k - 1], ar.at[k - 1],
             lambda k=k: place(*first(k), zl, zh, c), x >= y)
    order = []
    beside = [lambda: place(*second(1), zl, zh, c), lambda: place(*second(3), zl, zh, c)]
    for m in range(4):
        bx, by = first(4 - m) if m else (x, y)
        if m:
            arrived(sb.at[bx, by, c], as_.at[m - 1], ar.at[m - 1], bx >= by)
        for way in range(2):
            push(lambda bx=bx, by=by: sb.at[bx, by, c], lambda bx=bx, by=by: sb.at[bx, by, c],
                 ds.at[m, way], dr.at[m, way], beside[way], bx >= by)
        core_copy(m, bx, by)
        order.append((bx, by))
    shifted = lambda m, k: ((order[m][0] + c * k) % 4, (order[m][1] + (1 - c) * k) % 4)
    for m in range(4):
        for way in range(2):
            bx, by = shifted(m, 3 - 2 * way)
            arrived(sb.at[bx, by, c], ds.at[m, way], dr.at[m, way], bx >= by)
            part_of = lambda bx=bx, by=by, way=way: sb.at[bx, by, c, way * 4:way * 4 + 4]
            push(part_of, part_of, gs.at[m, way], gr.at[m, way], beside[way], bx >= by)
            core_copy(4 + (8 * way) + m, bx, by)
    arrived(theirs, fs, fr)
    for b in range(4):
        acc[b] = part[c, b] + theirs[b]
    for m in range(4):
        bx, by = shifted(m, 2)
        for way in range(2):
            arrived(sb.at[bx, by, c, way * 4:way * 4 + 4], gs.at[m, way], gr.at[m, way], bx >= by)
        core_copy(8 + m, bx, by)
    def half_copy():
        return pltpu.make_async_remote_copy(
            src_ref=ls2.at[1 - zh], dst_ref=lrz, send_sem=lhs, recv_sem=lhr,
            device_id=place(x, y, zl, 1 - zh, c), device_id_type=MESH,
        )


    def across_cores(row_block):
        for n in range(16):
            m, k = n % 4, n // 4
            bx = (x + 8 - (c * m + (1 - c) * k)) % 4
            by = (y + 8 - ((1 - c) * m + c * k)) % 4
            arrived(sb.at[bx, by, 1 - c], es.at[n], er.at[n], jnp.logical_and(by == row_block, bx >= by))

    for k in range(1, 4):
        push(lambda k=k: acc.at[(y + k) % 4], lambda k=k: lry.at[k - 1], lys.at[k - 1], lyr.at[k - 1],
             lambda k=k: place(x, (y + k) % 4, zl, zh, c))
    s[256:, :] = jnp.zeros((768, 1024), F32)

    def load(b):
        across_cores(b)

        def some(i, _):
            for k in range(2):
                for h in range(2):
                    at = pl.ds(pl.multiple_of(b * 256 + i * 32 + k * 16 + h * 8, 8), 8)
                    for a in range(b, 4):
                        span = slice(a * 256, a * 256 + 256)
                        if b == 0:
                            s[at, span] = sb[a, b, k, i, h]
                        else:
                            s[at, span] = s[at, span] + sb[a, b, k, i, h]
            return 0

        lax.fori_loop(0, 8, some, 0)

    load(0)
    row = lax.broadcasted_iota(jnp.int32, (128, 128), 0)
    col = lax.broadcasted_iota(jnp.int32, (128, 128), 1)
    eye = jnp.where(row == col, F32(1.0), F32(0.0))

    def block(j, _):
        for b in range(1, 4):
            pl.when(j == 2 * b)(functools.partial(load, b))

        dj = pl.ds(pl.multiple_of(j * 128, 128), 128)
        w[:, 0:128] = s[dj, dj]
        w[:, 128:256] = eye
        diagonal(w)
        t[dj, :] = w[:, 128:256]

        def across(k, _):
            dk = pl.ds(pl.multiple_of(k * 256, 256), 256)
            s[dj, dk] = dot(t[dj, :], s[dj, dk], 1, 0, HI)
            return 0

        lax.fori_loop((j + 1) // 2, 4, across, 0)
        s[dj, dj] = jnp.where(col >= row, w[:, 0:128], 0.0)

        def update(rows, start):
            left = s[dj, rows]

            def tile(k, _):
                dk = pl.ds(pl.multiple_of(k * 256, 256), 256)
                s[rows, dk] = s[rows, dk] - dot(left, s[dj, dk], 0, 0, HI)
                return 0

            lax.fori_loop(start, 4, tile, 0)

        @pl.when(j % 2 == 0)
        def _():
            update(pl.ds(pl.multiple_of(jnp.minimum(j + 1, 7) * 128, 128), 128), j // 2)

        def trailing(i, _):
            update(pl.ds(pl.multiple_of(i * 256, 256), 256), i)
            return 0

        lax.fori_loop(j // 2 + 1, 4, trailing, 0)

        @pl.when(j == 2)
        def _():
            for k in range(1, 4):
                arrived(lry.at[k - 1], lys.at[k - 1], lyr.at[k - 1])
            ls2[...] = acc[y] + lry[0] + lry[1] + lry[2]
            half_copy().start()

        return 0

    lax.fori_loop(0, 8, block, 0)
    half_copy().wait()
    gram = ls2[zh, 0] + lrz[0]
    r[...] = gram * gram - (ls2[zh, 1] + lrz[1])
    for j in range(8):
        a, b = j * 128, j * 128 + 128
        xj = dot(r[:, a:b], t[a:b, :], 1, 1, HI)
        panel[0, :, a:b] = xj
        if j < 7:
            r[:, b:] = r[:, b:] - dot(xj, s[a:b, b:], 1, 0, HI)
    tile = pl.ds(pl.multiple_of((d // 4) * 128, 128), 128)
    for j in range(8):
        flipped = s[j * 128:j * 128 + 128, tile].T
        for q in range(4):
            @pl.when(d % 4 == q)
            def _(q=q):
                lower[:, j * 128:j * 128 + 128] = jnp.where(d // 4 >= j, flipped[q * 32:q * 32 + 32, :], 0.0)
    for when, make in sent:
        if when is None:
            make().wait_send()
        else:
            pl.when(when)(lambda make=make: make().wait_send())


def whole_step(colloc, bc, factor, bf):
    D = pltpu.SemaphoreType.DMA
    whole = pl.BlockSpec(memory_space=pltpu.MemorySpace.HBM)
    return pl.pallas_call(
        panel_step,
        out_shape=[
            jax.ShapeDtypeStruct((32, 1024), F32),
            jax.ShapeDtypeStruct((1, 24, 1024), F32),
        ],
        in_specs=[whole] * 4,
        out_specs=[VMEM] * 2,
        scratch_shapes=[
            pltpu.VMEM((4, 2, 2, 24, 1024), F32),
            pltpu.VMEM((4, 4, 2, 8, 2, 8, 256), F32),
            pltpu.VMEM((1024, 1024), F32),
            pltpu.VMEM((1024, 128), F32),
            pltpu.VMEM((128, 256), F32),
            pltpu.VMEM((24, 1024), F32),
            pltpu.VMEM((32, 32, 500), jnp.bfloat16),
            pltpu.VMEM((32, 32, 512), F32),
            pltpu.VMEM((500, 384), jnp.bfloat16),
            pltpu.VMEM((384, 512), F32),
            pltpu.VMEM((2, 4, 2, 2, 24, 1024), F32),
            pltpu.VMEM((4, 2, 2, 24, 1024), F32),
            pltpu.VMEM((2, 4, 2, 2, 8, 256), F32),
            pltpu.VMEM((4, 2, 2, 8, 256), F32),
            pltpu.VMEM((4, 2, 2, 8, 256), F32),
            pltpu.VMEM((3, 2, 2, 8, 256), F32),
            pltpu.VMEM((2, 2, 8, 256), F32),
            pltpu.VMEM((2, 8, 256), F32),
            pltpu.VMEM((3, 2, 2, 24, 1024), F32),
            pltpu.VMEM((2, 2, 24, 1024), F32),
            pltpu.VMEM((2, 24, 1024), F32),
            D((4,)), D((3, 8)), D((3, 7, 2)), D((3, 2, 8)), D((3, 2, 8)),
            D, D, D((3,)), D((3,)), D, D, D((15,)), D((15,)), D((3,)), D((3,)),
            D((4, 2)), D((4, 2)), D((4, 2)), D((4, 2)), D((16,)), D((16,)), D, D,
            D((3,)), D((3,)), D, D,
        ],
        compiler_params=pltpu.CompilerParams(collective_id=0, has_side_effects=True, vmem_limit_bytes=60 * 2**20),
        name="panel_step",
    )(colloc, bc, factor, bf)


def on_device(colloc, block_colloc, factor, block_factor):
    return tuple(whole_step(colloc.T, block_colloc, factor, block_factor))


def solution(mesh):
    placed = (P("dev", "grp"), P("dev", "grp"), P("dev", "grp"), P("dev", "grp"))
    return jax.shard_map(
        on_device,
        mesh=mesh,
        in_specs=placed,
        out_specs=(P("dev", None), P("dev", "grp", None)),
        check_vma=False,
    )
```

```python
import functools

import jax
import jax.numpy as jnp
from jax import lax
from jax.experimental import pallas as pl
from jax.experimental.pallas import tpu as pltpu
from jax.sharding import PartitionSpec as P

DAMPING = 0.0625
HI = lax.Precision.HIGHEST
MESH = pl.DeviceIdType.MESH
F32 = jnp.float32
VMEM = pl.BlockSpec(memory_space=pltpu.VMEM)


def dot(a, b, ca, cb, precision=None):
    return lax.dot_general(a, b, (((ca,), (cb,)), ((), ())), precision=precision, preferred_element_type=F32)


def place(x, y, zl, zh, c):
    return {"grp": y * 4 + zh * 2 + c, "dev": x * 8 + zl}


def diagonal(w):
    wide = (8, 128)
    sub = lax.broadcasted_iota(jnp.int32, wide, 0)
    lane = lambda v, k: jnp.broadcast_to(v[:, k:k + 1], wide)
    line = lambda v, k: jnp.broadcast_to(v[k:k + 1, :], wide)
    r0, r1 = w[0:8, 0:128], w[0:8, 128:256]
    cols = [lane(r0, k) for k in range(8)]
    pivot = line(cols[0], 0)
    for g in range(16):
        lo = 8 * g
        more = g < 15
        if more:
            n0, n1 = w[lo + 8:lo + 16, 0:128], w[lo + 8:lo + 16, 128:256]
            left = [lane(n0, lo + k) for k in range(8)]
            ncols = [lane(n0, lo + 8 + k) for k in range(8)]
        scale = jnp.zeros(wide, F32)
        for k in range(8):
            inv = lax.rsqrt(pivot)
            inv2 = inv * inv
            if k < 7:
                e = line(cols[k + 1], k)
                pivot = line(cols[k + 1], k + 1) - (e * e) * inv2
            elif more:
                e = line(left[7], 0)
                pivot = line(ncols[0], 0) - (e * e) * inv2
            scale = jnp.where(sub == k, inv, scale)
            p0, p1 = line(r0, k), line(r1, k)
            if more:
                m2 = left[k] * inv2
            if k < 7:
                mult = jnp.where(sub > k, cols[k], 0.0) * inv2
                for j in range(k + 1, 8):
                    e = line(cols[j], k)
                    cols[j] = cols[j] - mult * e
                    if more:
                        left[j] = left[j] - m2 * e
                r0 = r0 - mult * p0
                r1 = r1 - mult * p1
            if more:
                for j in range(8):
                    ncols[j] = ncols[j] - m2 * line(left[k], j)
                n0 = n0 - m2 * p0
                n1 = n1 - m2 * p1
        u0, u1 = r0 * scale, r1 * scale
        w[lo:lo + 8, 0:128] = u0
        w[lo:lo + 8, 128:256] = u1
        first = g // 4 * 4
        reach = min(16, first + 6)
        if g + 2 < reach:
            flipped = u0.T
            q0 = [line(u0, k) for k in range(8)]
            q1 = [line(u1, k) for k in range(8)]
            for h in range(8 * g + 16, 8 * reach, 8):
                a0, a1 = w[h:h + 8, 0:128], w[h:h + 8, 128:256]
                for k in range(8):
                    m = jnp.broadcast_to(flipped[h:h + 8, k:k + 1], wide)
                    a0 = a0 - m * q0[k]
                    a1 = a1 - m * q1[k]
                w[h:h + 8, 0:128] = a0
                w[h:h + 8, 128:256] = a1
        if g == first + 3 and reach < 16:
            panel = w[8 * first:8 * first + 32, :]
            change = dot(panel[:, 0:128], panel, 0, 0, HI)
            w[8 * reach:128, :] = w[8 * reach:128, :] - change[8 * reach:128, :]
        if more:
            r0, r1, cols = n0, n1, ncols


def panel_step(colloc, bc, factor, bf, lower, panel, acc, sb, s, t, w, r, bca, bfa, tall, wide, part, theirs,
               dpart, rcore, dacc, ry, s2, rz, lone, lfwd, ltwo, ls2, lrz,
               ls, zr, zs, xr, xs, cs, cr, ys, yr, hs, hr, pr, ps, ar, as_, dr, ds, gr, gs, er, es, fs, fr,
               lys, lyr, lhs, lhr):
    g = lax.axis_index("grp")
    d = lax.axis_index("dev")
    y, zh, c = g // 4, (g // 2) % 2, g % 2
    x, zl = d // 8, d % 8
    sent = []

    local = [
        pltpu.make_async_copy(bc, bca.at[d], ls.at[0]),
        pltpu.make_async_copy(bf, bfa.at[d], ls.at[1]),
        pltpu.make_async_copy(colloc, tall, ls.at[2]),
        pltpu.make_async_copy(factor, wide, ls.at[3]),
    ]
    for copy in local:
        copy.start()

    def push(src, dst, ssem, rsem, to, when=None):
        def make():
            return pltpu.make_async_remote_copy(
                src_ref=src(), dst_ref=dst(), send_sem=ssem, recv_sem=rsem, device_id=to(), device_id_type=MESH
            )

        if when is None:
            make().start()
        else:
            pl.when(when)(lambda: make().start())
        sent.append((when, make))

    def arrived(ref, ssem, rsem, when=None):
        def wait():
            pltpu.make_async_remote_copy(
                src_ref=ref, dst_ref=ref, send_sem=ssem, recv_sem=rsem,
                device_id=place(x, y, zl, zh, 1 - c), device_id_type=MESH,
            ).wait_recv()

        if when is None:
            wait()
        else:
            pl.when(when)(wait)

    barrier = pltpu.get_barrier_semaphore()
    ring = [(zl + k % 8) % 8 for k in range(16)]
    half = [(zh + k // 8) % 2 for k in range(16)]
    peers = [place(x, y, zl, zh, 1 - c)]
    peers += [place(x, y, ring[k], half[k], c) for k in range(1, 16)]
    peers += [place((x + k) % 4, y, zl, zh, c) for k in range(1, 4)]
    peers += [place(x, (y + k) % 4, zl, zh, c) for k in range(1, 4)]
    for peer in peers:
        pl.semaphore_signal(barrier, inc=1, device_id=peer, device_id_type=MESH)
    pl.semaphore_wait(barrier, len(peers))

    chunks = [
        (bc, lambda slot: bca.at[slot]),
        (bf.at[0:16], lambda slot: bfa.at[slot, 0:16]),
        (bf.at[16:32], lambda slot: bfa.at[slot, 16:32]),
    ]
    whole = [(bc, lambda slot: bca.at[slot]), (bf, lambda slot: bfa.at[slot])]
    over = [lambda: place((x + 1) % 4, y, zl, zh, c), lambda: place((x + 3) % 4, y, zl, zh, c)]

    def to_x(src, own, when=None):
        for q, (mine, at) in enumerate(whole):
            for way in range(2):
                source = (lambda mine=mine: mine) if own else (lambda at=at: at(x * 8 + src))
                push(source, lambda at=at: at(x * 8 + src), xs.at[way, q, src], xr.at[way, q, src], over[way], when)

    def from_x(src):
        for q, (_, at) in enumerate(whole):
            for way in range(2):
                slot = ((x + 3 + 2 * way) % 4) * 8 + src
                arrived(at(slot), xs.at[way, q, src], xr.at[way, q, src])
                push(lambda at=at, slot=slot: at(slot), lambda at=at, slot=slot: at(slot),
                     xs.at[2, q, src], xr.at[2, q, src], over[way], (src % 2) == way)

    def from_far(src):
        for q, (_, at) in enumerate(whole):
            arrived(at(((x + 2) % 4) * 8 + src), xs.at[2, q, src], xr.at[2, q, src])

    for q, (own, at) in enumerate(chunks):
        for way, step in ((0, 1), (1, -1)):
            ok = (zl < 7) if step == 1 else (zl > 0)
            push(lambda own=own: own, lambda at=at: at(d), zs.at[q, 0, way], zr.at[q, zl],
                 lambda step=step: place(x, y, zl + step, zh, c), ok)
    to_x(zl, True)
    for hop in range(1, 8):
        for q, (own, at) in enumerate(chunks):
            for way, step in ((0, 1), (1, -1)):
                src = zl - step * hop
                inside = (src >= 0) if step == 1 else (src <= 7)
                more = (zl < 7) if step == 1 else (zl > 0)

                @pl.when(inside)
                def _(at=at, src=src, q=q):
                    arrived(at(x * 8 + src), zs.at[q, 0, 0], zr.at[q, src])

                if hop < 7:
                    push(lambda at=at, src=src: at(x * 8 + src), lambda at=at, src=src: at(x * 8 + src),
                         zs.at[q, hop, way], zr.at[q, src],
                         lambda step=step: place(x, y, zl + step, zh, c), jnp.logical_and(inside, more))
        for step in (1, -1):
            src = zl - step * hop
            to_x(src, False, (src >= 0) if step == 1 else (src <= 7))
        if hop == 2:
            from_x(zl)
    mine = pl.ds(x * 8, 8)
    local[0].wait()
    local[1].wait()
    from_far(zl)
    rows = [a * 8 + zl for a in range(4)]
    gram = dot(jnp.concatenate([bca[i] for i in rows], axis=0), bca[mine].reshape(256, 500), 1, 1)
    update = dot(jnp.concatenate([bfa[i] for i in rows], axis=0), bfa[mine].reshape(256, 512), 1, 1, HI)
    for a in range(4):
        for b in range(2):
            for e in range(2):
                lo = a * 32 + b * 16 + e * 8
                dpart[b, a, e, 0] = gram[lo:lo + 8]
                dpart[b, a, e, 1] = update[lo:lo + 8]
    push(lambda: dpart.at[1 - c], lambda: rcore, cs, cr, lambda: place(x, y, zl, zh, 1 - c))
    for k in range(1, 8):
        from_x((zl + k) % 8)
    arrived(rcore, cs, cr)
    dacc[...] = dpart[c] + rcore[...]
    for k in range(1, 4):
        push(lambda k=k: dacc.at[(y + k) % 4], lambda k=k: ry.at[k - 1], ys.at[k - 1], yr.at[k - 1],
             lambda k=k: place(x, (y + k) % 4, zl, zh, c))
    for k in range(1, 4):
        arrived(ry.at[k - 1], ys.at[k - 1], yr.at[k - 1])
    s2[...] = dacc[y] + ry[0] + ry[1] + ry[2]
    push(lambda: s2.at[1 - zh], lambda: rz, hs, hr, lambda: place(x, y, zl, 1 - zh, c))
    for k in range(1, 8):
        from_far((zl + k) % 8)
    local[2].wait()
    local[3].wait()
    for b in range(3):
        gram = dot(tall[:, 128 * b:128 * b + 128], bca[...].reshape(1024, 500), 0, 1)
        for n in range(16):
            lo, hi = max(24 * n, 128 * b), min(24 * n + 24, 128 * b + 128)
            if lo < hi:
                part[n % 2, n // 4, (n // 2) % 2, 0, lo - 24 * n:hi - 24 * n] = gram[lo - 128 * b:hi - 128 * b]

    def products(b):
        update = dot(wide[96 * b:96 * b + 96, :], bfa[...].reshape(1024, 512), 1, 1, HI)
        for h in range(2):
            for k in range(2):
                lo = (h * 2 + k) * 24
                part[k, b, h, 1] = update[lo:lo + 24]

    products(0)
    products(1)
    arrived(rz, hs, hr)
    total = s2[zh] + rz[...]
    row = y * 256 + zl * 32 + c * 16 + zh * 8 + lax.broadcasted_iota(jnp.int32, (8, 256), 0)
    col = x * 256 + lax.broadcasted_iota(jnp.int32, (8, 256), 1)
    sb[x, y, c, zl, zh] = total[0] * total[0] + jnp.where(row == col, F32(DAMPING), F32(0.0)) - total[1]
    for k in range(1, 16):
        push(lambda: sb.at[x, y, c, zl, zh], lambda: sb.at[x, y, c, zl, zh], ps.at[k - 1], pr.at[k - 1],
             lambda k=k: place(x, y, ring[k], half[k], c), x >= y)
    products(2)
    products(3)
    push(lambda: part.at[1 - c], lambda: theirs, fs, fr, lambda: place(x, y, zl, zh, 1 - c))
    for k in range(1, 16):
        back_l, back_h = (zl + 8 - k % 8) % 8, (zh + k // 8) % 2
        arrived(sb.at[x, y, c, back_l, back_h], ps.at[k - 1], pr.at[k - 1], x >= y)
    first = lambda k: ((x + (1 - c) * k) % 4, (y + c * k) % 4)
    second = lambda k: ((x + c * k) % 4, (y + (1 - c) * k) % 4)

    def core_copy(n, bx, by):
        push(lambda: sb.at[bx, by, c], lambda: sb.at[bx, by, c], es.at[n], er.at[n],
             lambda: place(x, y, zl, zh, 1 - c), bx >= by)

    for k in range(1, 4):
        push(lambda: sb.at[x, y, c], lambda: sb.at[x, y, c], as_.at[k - 1], ar.at[k - 1],
             lambda k=k: place(*first(k), zl, zh, c), x >= y)
    order = []
    beside = [lambda: place(*second(1), zl, zh, c), lambda: place(*second(3), zl, zh, c)]
    for m in range(4):
        bx, by = first(4 - m) if m else (x, y)
        if m:
            arrived(sb.at[bx, by, c], as_.at[m - 1], ar.at[m - 1], bx >= by)
        for way in range(2):
            push(lambda bx=bx, by=by: sb.at[bx, by, c], lambda bx=bx, by=by: sb.at[bx, by, c],
                 ds.at[m, way], dr.at[m, way], beside[way], bx >= by)
        core_copy(m, bx, by)
        order.append((bx, by))
    shifted = lambda m, k: ((order[m][0] + c * k) % 4, (order[m][1] + (1 - c) * k) % 4)
    for m in range(4):
        for way in range(2):
            bx, by = shifted(m, 3 - 2 * way)
            arrived(sb.at[bx, by, c], ds.at[m, way], dr.at[m, way], bx >= by)
            part_of = lambda bx=bx, by=by, way=way: sb.at[bx, by, c, way * 4:way * 4 + 4]
            push(part_of, part_of, gs.at[m, way], gr.at[m, way], beside[way], bx >= by)
            core_copy(4 + (8 * way) + m, bx, by)
    arrived(theirs, fs, fr)
    for b in range(4):
        acc[b] = part[c, b] + theirs[b]
    for m in range(4):
        bx, by = shifted(m, 2)
        for way in range(2):
            arrived(sb.at[bx, by, c, way * 4:way * 4 + 4], gs.at[m, way], gr.at[m, way], bx >= by)
        core_copy(8 + m, bx, by)
    def half_copy():
        return pltpu.make_async_remote_copy(
            src_ref=ls2.at[1 - zh], dst_ref=lrz, send_sem=lhs, recv_sem=lhr,
            device_id=place(x, y, zl, 1 - zh, c), device_id_type=MESH,
        )


    def across_cores(row_block):
        for n in range(16):
            m, k = n % 4, n // 4
            bx = (x + 8 - (c * m + (1 - c) * k)) % 4
            by = (y + 8 - ((1 - c) * m + c * k)) % 4
            arrived(sb.at[bx, by, 1 - c], es.at[n], er.at[n], jnp.logical_and(by == row_block, bx >= by))

    pair, mirror = y + 1 - 2 * (y % 2), 3 - y
    meet = [(pair, mirror), (mirror, pair)]

    def y_copy(src, dst, n, to):
        return pltpu.make_async_remote_copy(
            src_ref=src, dst_ref=dst, send_sem=lys.at[n], recv_sem=lyr.at[n],
            device_id=place(x, to, zl, zh, c), device_id_type=MESH,
        )

    def one(i, k):
        near, far = meet[i]
        beyond = 3 - near if i == 0 else near + 1 - 2 * (near % 2)
        return y_copy(acc.at[near if k == 0 else beyond, i], lone.at[i, k], 2 * i + k, near)

    def two(i):
        return y_copy(lfwd.at[i], ltwo.at[i], 4 + i, meet[i][1])

    s[256:, :] = jnp.zeros((768, 1024), F32)

    def load(b):
        across_cores(b)

        def some(i, _):
            for k in range(2):
                for h in range(2):
                    at = pl.ds(pl.multiple_of(b * 256 + i * 32 + k * 16 + h * 8, 8), 8)
                    for a in range(b, 4):
                        span = slice(a * 256, a * 256 + 256)
                        if b == 0:
                            s[at, span] = sb[a, b, k, i, h]
                        else:
                            s[at, span] = s[at, span] + sb[a, b, k, i, h]
            return 0

        lax.fori_loop(0, 8, some, 0)

    load(0)
    row = lax.broadcasted_iota(jnp.int32, (128, 128), 0)
    col = lax.broadcasted_iota(jnp.int32, (128, 128), 1)
    eye = jnp.where(row == col, F32(1.0), F32(0.0))

    def block(j, _):
        for b in range(1, 4):
            pl.when(j == 2 * b)(functools.partial(load, b))

        dj = pl.ds(pl.multiple_of(j * 128, 128), 128)
        w[:, 0:128] = s[dj, dj]
        w[:, 128:256] = eye
        diagonal(w)
        t[dj, :] = w[:, 128:256]

        def across(k, _):
            dk = pl.ds(pl.multiple_of(k * 256, 256), 256)
            s[dj, dk] = dot(t[dj, :], s[dj, dk], 1, 0, HI)
            return 0

        lax.fori_loop((j + 1) // 2, 4, across, 0)
        s[dj, dj] = jnp.where(col >= row, w[:, 0:128], 0.0)

        def update(rows, start):
            left = s[dj, rows]

            def tile(k, _):
                dk = pl.ds(pl.multiple_of(k * 256, 256), 256)
                s[rows, dk] = s[rows, dk] - dot(left, s[dj, dk], 0, 0, HI)
                return 0

            lax.fori_loop(start, 4, tile, 0)

        @pl.when(j % 2 == 0)
        def _():
            update(pl.ds(pl.multiple_of(jnp.minimum(j + 1, 7) * 128, 128), 128), j // 2)

        def trailing(i, _):
            update(pl.ds(pl.multiple_of(i * 256, 256), 256), i)
            return 0

        lax.fori_loop(j // 2 + 1, 4, trailing, 0)

        @pl.when(j == 1)
        def _():
            for i in range(2):
                for k in range(2):
                    one(i, k).start()

        @pl.when(j == 3)
        def _():
            for i in range(2):
                for k in range(2):
                    one(i, k).wait()
                lfwd[i] = acc[meet[i][1], i] + lone[i, 1]
                two(i).start()

        @pl.when(j == 4)
        def _():
            for i in range(2):
                two(i).wait()
                ls2[i] = acc[y, i] + lone[i, 0] + ltwo[i]
            half_copy().start()

        return 0

    lax.fori_loop(0, 8, block, 0)
    half_copy().wait()
    gram = ls2[zh, 0] + lrz[0]
    r[...] = gram * gram - (ls2[zh, 1] + lrz[1])
    for j in range(8):
        a, b = j * 128, j * 128 + 128
        xj = dot(r[:, a:b], t[a:b, :], 1, 1, HI)
        panel[0, :, a:b] = xj
        if j < 7:
            r[:, b:] = r[:, b:] - dot(xj, s[a:b, b:], 1, 0, HI)
    tile = pl.ds(pl.multiple_of((d // 4) * 128, 128), 128)
    for j in range(8):
        flipped = s[j * 128:j * 128 + 128, tile].T
        for q in range(4):
            @pl.when(d % 4 == q)
            def _(q=q):
                lower[:, j * 128:j * 128 + 128] = jnp.where(d // 4 >= j, flipped[q * 32:q * 32 + 32, :], 0.0)
    for when, make in sent:
        if when is None:
            make().wait_send()
        else:
            pl.when(when)(lambda make=make: make().wait_send())


def whole_step(colloc, bc, factor, bf):
    D = pltpu.SemaphoreType.DMA
    whole = pl.BlockSpec(memory_space=pltpu.MemorySpace.HBM)
    return pl.pallas_call(
        panel_step,
        out_shape=[
            jax.ShapeDtypeStruct((32, 1024), F32),
            jax.ShapeDtypeStruct((1, 24, 1024), F32),
        ],
        in_specs=[whole] * 4,
        out_specs=[VMEM] * 2,
        scratch_shapes=[
            pltpu.VMEM((4, 2, 2, 24, 1024), F32),
            pltpu.VMEM((4, 4, 2, 8, 2, 8, 256), F32),
            pltpu.VMEM((1024, 1024), F32),
            pltpu.VMEM((1024, 128), F32),
            pltpu.VMEM((128, 256), F32),
            pltpu.VMEM((24, 1024), F32),
            pltpu.VMEM((32, 32, 500), jnp.bfloat16),
            pltpu.VMEM((32, 32, 512), F32),
            pltpu.VMEM((500, 384), jnp.bfloat16),
            pltpu.VMEM((384, 512), F32),
            pltpu.VMEM((2, 4, 2, 2, 24, 1024), F32),
            pltpu.VMEM((4, 2, 2, 24, 1024), F32),
            pltpu.VMEM((2, 4, 2, 2, 8, 256), F32),
            pltpu.VMEM((4, 2, 2, 8, 256), F32),
            pltpu.VMEM((4, 2, 2, 8, 256), F32),
            pltpu.VMEM((3, 2, 2, 8, 256), F32),
            pltpu.VMEM((2, 2, 8, 256), F32),
            pltpu.VMEM((2, 8, 256), F32),
            pltpu.VMEM((2, 2, 2, 24, 1024), F32),
            pltpu.VMEM((2, 2, 24, 1024), F32),
            pltpu.VMEM((2, 2, 24, 1024), F32),
            pltpu.VMEM((2, 2, 24, 1024), F32),
            pltpu.VMEM((2, 24, 1024), F32),
            D((4,)), D((3, 8)), D((3, 7, 2)), D((3, 2, 8)), D((3, 2, 8)),
            D, D, D((3,)), D((3,)), D, D, D((15,)), D((15,)), D((3,)), D((3,)),
            D((4, 2)), D((4, 2)), D((4, 2)), D((4, 2)), D((16,)), D((16,)), D, D,
            D((6,)), D((6,)), D, D,
        ],
        compiler_params=pltpu.CompilerParams(collective_id=0, has_side_effects=True, vmem_limit_bytes=60 * 2**20),
        name="panel_step",
    )(colloc, bc, factor, bf)


def on_device(colloc, block_colloc, factor, block_factor):
    return tuple(whole_step(colloc.T, block_colloc, factor, block_factor))


def solution(mesh):
    placed = (P("dev", "grp"), P("dev", "grp"), P("dev", "grp"), P("dev", "grp"))
    return jax.shard_map(
        on_device,
        mesh=mesh,
        in_specs=placed,
        out_specs=(P("dev", None), P("dev", "grp", None)),
        check_vma=False,
    )
```
